256 devices in a mesh: freq: 16 (over z, core), seg: 16 (over x, y).
Axes of the slice: x: 4, y: 4, z: 8, core: 2. Of those that a mesh axis runs over, the one named last changes fastest.
Arguments:
- propagators: float32 [16, 256, 2, 128, 128], P('seg', 'freq'), may hold values from -2 to 2, as said below
- source_modes: float32 [256, 2, 128], P('freq'), may hold values from -6 to 6
Outputs:
- amplitudes: float32 [16, 256, 2, 128], P('seg', 'freq')
- waveforms: float32 [256, 16, 128], P('freq', 'seg')
The draws below stay inside these ranges and needn't reach their ends.
Inputs may be any that keep to these rules, and one draw needn't show every extreme that they name: `propagators`: each propagator is a diagonal of unit phases times (the identity plus a dense complex coupling part).
All inputs are finite; a program needn't handle non-finite values.
Results may differ from the reference program's by a relative error of at most 0.00019.
Values sent between devices are 32-bit elements; how exact they have to be, the bound alone decides.
A program may use at most 64 MiB of HBM per device.

```python
import jax
import jax.numpy as jnp
from jax import lax

MODES = 128
FREQS = 256
TIMES = 256
SEGMENTS = 16


def draw_propagators(key, part):
    key_phase = jax.random.fold_in(key, 11)
    key_couple = jax.random.fold_in(key, 12)
    theta = jax.random.uniform(key_phase, (SEGMENTS, FREQS, MODES), jnp.float32, -jnp.pi, jnp.pi)
    spread = 0.35 / jnp.sqrt(jnp.float32(MODES))
    coupling = jax.random.normal(key_couple, (SEGMENTS, FREQS, 2, MODES, MODES), jnp.float32) * spread
    base_real = coupling[:, :, 0] + jnp.eye(MODES, dtype=jnp.float32)
    base_imag = coupling[:, :, 1]
    cosines = jnp.cos(theta)[..., None]
    sines = jnp.sin(theta)[..., None]
    prop_real = cosines * base_real - sines * base_imag
    prop_imag = sines * base_real + cosines * base_imag
    return jnp.stack([prop_real, prop_imag], axis=2)


def block_scale(key, dims, pieces, low, high):
    factor_of, own = 1.0, jax.random.fold_in(key, 6)
    for dim, parts in pieces:
        draws = jnp.exp(jax.random.uniform(jax.random.fold_in(own, dim), (parts,), jnp.float32, low / len(pieces), high / len(pieces)))
        factor_of = factor_of * jnp.repeat(draws, dims[dim] // parts).reshape([-1 if axis == dim else 1 for axis in range(len(dims))])
    return factor_of


def noise(rng, extent, scale, limit, shards=(), kind=jnp.bfloat16):
    values = jax.random.normal(rng, extent, jnp.float32) * scale
    if len(shards) > 0:
        values = block_scale(rng, extent, shards, -0.22, 0.18) * values
    return jnp.clip(values, min=-limit, max=limit).astype(kind)


def setup_inputs(seed: int = 0) -> dict:
    arg_keys = jax.random.split(jax.random.key(seed), 3)
    propagators = draw_propagators(jax.random.fold_in(arg_keys[2], 71), 0)
    source_modes = noise(arg_keys[1], (FREQS, 2, MODES), 1.0, 6.0, ((0, 16),), jnp.float32)
    return {"propagators": propagators, "source_modes": source_modes}


def apply_modes(prop, vec):
    hi = lax.Precision.HIGHEST
    real_part = jnp.einsum('fij,fj->fi', prop[:, 0], vec[:, 0], precision=hi) - jnp.einsum('fij,fj->fi', prop[:, 1], vec[:, 1], precision=hi)
    imag_part = jnp.einsum('fij,fj->fi', prop[:, 0], vec[:, 1], precision=hi) + jnp.einsum('fij,fj->fi', prop[:, 1], vec[:, 0], precision=hi)
    return jnp.stack([real_part, imag_part], axis=1)

def reference(propagators, source_modes):

    def advance(carry, prop):
        nxt = apply_modes(prop, carry)
        return (nxt, nxt)
    final, amplitudes = lax.scan(advance, source_modes, propagators)
    tgrid = jnp.arange(TIMES, dtype=jnp.int32)
    fgrid = jnp.arange(FREQS, dtype=jnp.int32)
    phase = (tgrid[:, None] * fgrid[None, :] % TIMES).astype(jnp.float32) * (2.0 * jnp.pi / TIMES)
    table = jnp.concatenate([jnp.cos(phase), -jnp.sin(phase)], axis=1) / jnp.sqrt(jnp.float32(TIMES))

    def synth(segment_amps):
        stacked = jnp.concatenate([segment_amps[:, 0], segment_amps[:, 1]], axis=0)
        return jnp.dot(table, stacked, precision=lax.Precision.HIGHEST)
    waves = lax.map(synth, amplitudes)
    return (amplitudes, jnp.transpose(waves, (1, 0, 2)))
```

```python
import functools

import jax
import jax.numpy as jnp
import numpy as np
from jax import lax
from jax.experimental import pallas as pl
from jax.experimental.pallas import tpu as pltpu
from jax.sharding import PartitionSpec as P

MESH = pl.DeviceIdType.MESH
F32 = jnp.float32


def ring_offsets(side):
    half = side // 2
    steps = [d if d <= half else d - side for d in range(side)]
    pairs = [(dx, dy) for dx in steps for dy in steps if (dx, dy) != (0, 0)]
    return sorted(pairs, key=lambda p: -(abs(p[0]) + abs(p[1])))


def kernel(n_seg, n_freq, prop, src, amp_out, wave_out, mats, own, amp, part, got, table,
           psend, precv, asend, arecv, wsend, wrecv, local_sem):
    side = 4
    seg = lax.axis_index("seg")
    freq = lax.axis_index("freq")
    modes = mats.shape[-1]
    rows = wave_out.shape[0]
    n_time = rows * n_freq
    x0, y0 = seg // side, lax.rem(seg, side)

    barrier = pltpu.get_barrier_semaphore()
    for k in range(1, n_seg):
        pl.semaphore_signal(barrier, 1, device_id=(freq, lax.rem(seg + k, n_seg)), device_id_type=MESH)
    for k in range(1, n_freq):
        pl.semaphore_signal(barrier, 1, device_id=(lax.rem(freq + k, n_freq), seg), device_id_type=MESH)

    keep = pltpu.make_async_copy(prop.at[0, seg], mats.at[seg], precv.at[seg])
    keep.start()
    t = lax.broadcasted_iota(jnp.int32, (n_time, n_seg), 0)
    f = lax.broadcasted_iota(jnp.int32, (n_time, n_seg), 1) + freq * n_seg
    phase = lax.rem(t * f, n_time).astype(F32) * (2.0 * np.pi / n_time)
    scale = 1.0 / np.sqrt(np.float32(n_time))
    table[0] = jnp.cos(phase) * scale
    table[1] = jnp.sin(phase) * -scale

    pl.semaphore_wait(barrier, n_seg + n_freq - 2)

    sends = []
    for i, (dx, dy) in enumerate(ring_offsets(side)):
        to = lax.rem(x0 + dx + side, side) * side + lax.rem(y0 + dy + side, side)
        copy = pltpu.make_async_remote_copy(
            prop.at[0, to], mats.at[seg], psend.at[i], precv.at[seg],
            device_id=(freq, to), device_id_type=MESH)
        copy.start()
        sends.append(copy)

    eye = lax.broadcasted_iota(jnp.int32, (modes, modes), 0) == lax.broadcasted_iota(
        jnp.int32, (modes, modes), 1)

    def to_row(column):
        return jnp.sum(jnp.where(eye, column, 0.0), axis=0, keepdims=True)

    def amp_copy(s):
        return pltpu.make_async_remote_copy(
            own.at[s], amp.at[seg], asend.at[s], arecv,
            device_id=(freq, s), device_id_type=MESH)

    def step(s, vec):
        re, im = vec
        pltpu.make_async_copy(mats.at[s], mats.at[s], precv.at[s]).wait()
        p_re, p_im = mats[s, 0], mats[s, 1]
        n_re = to_row(jnp.sum(p_re * re - p_im * im, axis=1, keepdims=True))
        n_im = to_row(jnp.sum(p_re * im + p_im * re, axis=1, keepdims=True))
        own[s, 0:1, :] = n_re
        own[s, 1:2, :] = n_im

        @pl.when(s == seg)
        def _():
            amp[s, 0:1, :] = n_re
            amp[s, 1:2, :] = n_im

        @pl.when(s != seg)
        def _():
            amp_copy(s).start()

        return n_re, n_im

    lax.fori_loop(0, n_seg, step, (src[seg, 0:1, :], src[seg, 1:2, :]))

    pltpu.make_async_copy(amp.at[pl.ds(0, n_seg - 1)], amp.at[pl.ds(0, n_seg - 1)], arecv).wait()
    amp_out[0] = amp[...]
    a_re, a_im = amp[:, 0, :], amp[:, 1, :]
    hi = lax.Precision.HIGHEST
    part[...] = (
        jnp.dot(table[0], a_re, precision=hi, preferred_element_type=F32)
        + jnp.dot(table[1], a_im, precision=hi, preferred_element_type=F32)
    ).reshape(n_freq, rows, modes)

    outs = []
    for k in range(1, n_freq):
        to = lax.rem(freq + k, n_freq)
        copy = pltpu.make_async_remote_copy(
            part.at[to], got.at[k - 1], wsend.at[k - 1], wrecv,
            device_id=(to, seg), device_id_type=MESH)
        copy.start()
        outs.append(copy)
    pltpu.make_async_copy(got, got, wrecv).wait()
    wave_out[:, 0, :] = part[freq] + jnp.sum(got[...], axis=0)

    for copy in sends:
        copy.wait_send()
    for copy in outs:
        copy.wait_send()

    def drain(s, carry):
        @pl.when(s != seg)
        def _():
            amp_copy(s).wait_send()

        return carry

    lax.fori_loop(0, n_seg, drain, 0)


def local(propagators, source_modes):
    n_seg, n_freq = lax.axis_size("seg"), lax.axis_size("freq")
    _, group, _, modes, _ = propagators.shape
    vmem = pl.BlockSpec(memory_space=pltpu.VMEM)
    dma = pltpu.SemaphoreType.DMA
    return pl.pallas_call(
        functools.partial(kernel, n_seg, n_freq),
        out_shape=(
            jax.ShapeDtypeStruct((1, group, 2, modes), F32),
            jax.ShapeDtypeStruct((group, 1, modes), F32),
        ),
        in_specs=[pl.BlockSpec(memory_space=pl.ANY), vmem],
        out_specs=(vmem, vmem),
        scratch_shapes=[
            pltpu.VMEM((n_seg, 2, modes, modes), F32),
            pltpu.VMEM((n_seg, 2, modes), F32),
            pltpu.VMEM((n_seg, 2, modes), F32),
            pltpu.VMEM((n_freq, group, modes), F32),
            pltpu.VMEM((n_freq - 1, group, modes), F32),
            pltpu.VMEM((2, n_freq * group, n_seg), F32),
            dma((n_seg - 1,)),
            dma((n_seg,)),
            dma((n_seg,)),
            dma,
            dma((n_freq - 1,)),
            dma,
            dma,
        ],
        compiler_params=pltpu.CompilerParams(
            collective_id=0, has_side_effects=True, vmem_limit_bytes=48 << 20
        ),
    )(propagators, source_modes)


def solution(mesh):
    placed = (P("seg", "freq", None, None, None), P("freq", None, None))
    return jax.shard_map(
        local,
        mesh=mesh,
        in_specs=placed,
        out_specs=(P("seg", "freq", None, None), P("freq", "seg", None)),
        check_vma=False,
    )
```

```python
import functools

import jax
import jax.numpy as jnp
import numpy as np
from jax import lax
from jax.experimental import pallas as pl
from jax.experimental.pallas import tpu as pltpu
from jax.sharding import PartitionSpec as P

MESH = pl.DeviceIdType.MESH
F32 = jnp.float32
BF16 = jnp.bfloat16
SIDE = 4
CORES = 2
PLANE = (
    (2, 2), (1, 2), (2, 1), (-1, 2), (2, -1), (1, 1), (-1, -1), (1, -1), (-1, 1),
    (2, 0), (0, 2), (1, 0), (0, 1), (-1, 0), (0, -1),
)
PIECES = 4


def split3(value):
    hi = value.astype(BF16)
    rest = value - hi.astype(F32)
    mid = rest.astype(BF16)
    return hi, mid, (rest - mid.astype(F32)).astype(BF16)


def kernel(n_seg, n_freq, prop, src, amp_out, wave_out, mats, own, amp, part, got, table, first,
           psend, precv, asend, arecv, wsend, wrecv, fsem, line_sem):
    seg = lax.axis_index("seg")
    freq = lax.axis_index("freq")
    modes = mats.shape[-1]
    rows = wave_out.shape[0]
    n_time = rows * n_freq
    x0, y0 = seg // SIDE, lax.rem(seg, SIDE)
    depth = n_freq // CORES
    z0, core = freq // CORES, lax.rem(freq, CORES)

    def at(offset):
        dx, dy = offset
        return lax.rem(x0 + dx + SIDE, SIDE) * SIDE + lax.rem(y0 + dy + SIDE, SIDE)

    def along(dz, dc):
        return lax.rem(z0 + dz + depth, depth) * CORES + lax.rem(core + dc, CORES)

    plane = [at(offset) for offset in PLANE]
    near_line = [along(0, 1), along(1, 0), along(-1, 0)]

    barrier = pltpu.get_barrier_semaphore()
    for to in plane:
        pl.semaphore_signal(barrier, 1, device_id=(freq, to), device_id_type=MESH)
    for to in near_line:
        pl.semaphore_signal(barrier, 1, device_id=(to, seg), device_id_type=MESH)

    keep = pltpu.make_async_copy(prop.at[0, seg], mats.at[seg], precv.at[seg])
    keep.start()
    begin = pltpu.make_async_copy(src.at[seg], first, fsem)
    begin.start()

    pl.semaphore_wait(barrier, len(plane) + len(near_line))

    length = modes // PIECES
    for p in range(PIECES):
        for to in plane:
            cut = pl.ds(p * length, length)
            pltpu.make_async_remote_copy(
                prop.at[0, to, :, cut], mats.at[seg, :, cut], psend, precv.at[seg],
                device_id=(freq, to), device_id_type=MESH).start()

    width = CORES * n_seg
    t = lax.broadcasted_iota(jnp.int32, (n_time, modes), 0)
    lane = lax.broadcasted_iota(jnp.int32, (n_time, modes), 1)
    column, block = lax.rem(lane, width), lane // width
    f = column // 2 + freq * n_seg
    phase = lax.rem(t * f, n_time).astype(F32) * (2.0 * np.pi / n_time)
    scale = 1.0 / np.sqrt(np.float32(n_time))
    twiddle = jnp.where(lax.rem(column, 2) == 0, jnp.cos(phase), -jnp.sin(phase)) * scale
    t_hi, t_mid, t_lo = (v.astype(F32) for v in split3(twiddle))
    zero = jnp.zeros_like(twiddle)
    table[:, :modes] = jnp.where(block < 2, t_hi, t_mid).astype(BF16)
    table[:, modes:] = jnp.where(
        block == 0, t_hi, jnp.where(block == 1, t_lo, zero)).astype(BF16)

    rounds = depth // 2
    for r in range(rounds):
        for to in near_line:
            pl.semaphore_signal(line_sem.at[r], 1, device_id=(to, seg), device_id_type=MESH)
        pl.semaphore_wait(line_sem.at[r], len(near_line))

    eye = lax.broadcasted_iota(jnp.int32, (modes, modes), 0) == lax.broadcasted_iota(
        jnp.int32, (modes, modes), 1)

    def to_row(value):
        return jnp.sum(jnp.where(eye, value, 0.0), axis=0, keepdims=True)

    def amp_copy(s):
        return pltpu.make_async_remote_copy(
            own.at[s], amp.at[seg], asend.at[s], arecv,
            device_id=(freq, s), device_id_type=MESH)

    def step(s, vec):
        re, im = vec
        pltpu.make_async_copy(mats.at[s], mats.at[s], precv.at[s]).wait()
        p_re, p_im = mats[s, 0], mats[s, 1]
        n_re = to_row(jnp.sum(p_re * re - p_im * im, axis=1, keepdims=True))
        n_im = to_row(jnp.sum(p_re * im + p_im * re, axis=1, keepdims=True))
        own[s, 0:1, :] = n_re
        own[s, 1:2, :] = n_im

        @pl.when(s == seg)
        def _():
            amp[s, 0:1, :] = n_re
            amp[s, 1:2, :] = n_im

        @pl.when(s != seg)
        def _():
            amp_copy(s).start()

        return n_re, n_im

    begin.wait()
    lax.fori_loop(0, n_seg, step, (first[0:1, :], first[1:2, :]))

    pltpu.make_async_copy(amp.at[pl.ds(0, n_seg - 1)], amp.at[pl.ds(0, n_seg - 1)], arecv).wait()
    a_hi, a_mid, a_lo = split3(amp[...].reshape(2 * n_seg, modes))
    none = jnp.zeros_like(a_hi)
    stacked = jnp.concatenate([a_hi, a_mid, a_hi, a_mid, a_lo, a_hi, none, none], axis=0)
    part[...] = jnp.dot(table[...], stacked, preferred_element_type=F32).reshape(
        n_freq, rows, modes)

    outs = []
    half = depth // 2
    for dz in sorted(range(1 - half, half + 1), key=lambda d: -abs(d)):
        for dc in range(CORES):
            if (dz, dc) == (0, 0):
                continue
            to = along(dz, dc)
            i = len(outs)
            copy = pltpu.make_async_remote_copy(
                part.at[to], got.at[i], wsend.at[i], wrecv,
                device_id=(to, seg), device_id_type=MESH)
            copy.start()
            outs.append(copy)

    amp_out[0] = amp[...]
    sent = mats.at[pl.ds(0, n_seg - 1)]
    pltpu.make_async_copy(sent, sent, psend).wait()

    def drain(s, carry):
        @pl.when(s != seg)
        def _():
            amp_copy(s).wait_send()

        return carry

    lax.fori_loop(0, n_seg, drain, 0)
    pltpu.make_async_copy(got, got, wrecv).wait()
    wave_out[:, 0, :] = part[freq] + jnp.sum(got[...], axis=0)
    for copy in outs:
        copy.wait_send()


def local(propagators, source_modes):
    n_seg, n_freq = lax.axis_size("seg"), lax.axis_size("freq")
    _, group, _, modes, _ = propagators.shape
    dma, plain = pltpu.SemaphoreType.DMA, pltpu.SemaphoreType.REGULAR
    amps, waves = pl.pallas_call(
        functools.partial(kernel, n_seg, n_freq),
        out_shape=(
            jax.ShapeDtypeStruct((1, group, 2, modes), F32),
            jax.ShapeDtypeStruct((group, 1, modes), F32),
        ),
        in_specs=[pl.BlockSpec(memory_space=pltpu.HBM)] * 2,
        out_specs=(pl.BlockSpec(memory_space=pltpu.VMEM),) * 2,
        scratch_shapes=[
            pltpu.VMEM((n_seg, 2, modes, modes), F32),
            pltpu.VMEM((n_seg, 2, modes), F32),
            pltpu.VMEM((n_seg, 2, modes), F32),
            pltpu.VMEM((n_freq, group, modes), F32),
            pltpu.VMEM((n_freq - 1, group, modes), F32),
            pltpu.VMEM((n_freq * group, 2 * modes), BF16),
            pltpu.VMEM((2, modes), F32),
            dma,
            dma((n_seg,)),
            dma((n_seg,)),
            dma,
            dma((n_freq - 1,)),
            dma,
            dma,
            plain((n_freq // CORES // 2,)),
        ],
        compiler_params=pltpu.CompilerParams(
            collective_id=0, has_side_effects=True, vmem_limit_bytes=54500 << 10
        ),
    )(*(pltpu.with_memory_space_constraint(v, pltpu.HBM) for v in (propagators, source_modes)))

    def hand_on(a, w, a_out, w_out):
        a_out[...] = a[...]
        w_out[...] = w[...]

    return pl.pallas_call(
        hand_on,
        out_shape=(
            jax.ShapeDtypeStruct(amps.shape, F32),
            jax.ShapeDtypeStruct(waves.shape, F32),
        ),
        compiler_params=pltpu.CompilerParams(vmem_limit_bytes=4 << 20),
    )(amps, waves)


def solution(mesh):
    placed = (P("seg", "freq", None, None, None), P("freq", None, None))
    return jax.shard_map(
        local,
        mesh=mesh,
        in_specs=placed,
        out_specs=(P("seg", "freq", None, None), P("freq", "seg", None)),
        check_vma=False,
    )
```

```python
import functools

import jax
import jax.numpy as jnp
import numpy as np
from jax import lax
from jax.experimental import pallas as pl
from jax.experimental.pallas import tpu as pltpu
from jax.sharding import PartitionSpec as P

MESH = pl.DeviceIdType.MESH
F32 = jnp.float32
BF16 = jnp.bfloat16
SIDE = 4
CORES = 2
PLANE = (
    (2, 2), (1, 2), (2, 1), (-1, 2), (2, -1), (1, 1), (-1, -1), (1, -1), (-1, 1),
    (2, 0), (0, 2), (1, 0), (0, 1), (-1, 0), (0, -1),
)
HEAD_NEAR = 96
HEAD_SECOND = 64


def split3(value):
    hi = value.astype(BF16)
    rest = value - hi.astype(F32)
    mid = rest.astype(BF16)
    return hi, mid, (rest - mid.astype(F32)).astype(BF16)


def kernel(n_seg, n_freq, prop, src, amp_out, wave_out, mats, own, amp, part, got, table, first,
           psend, precv, asend, arecv, wsend, wrecv, fsem, line_sem, plane_sem):
    seg = lax.axis_index("seg")
    freq = lax.axis_index("freq")
    modes = mats.shape[-1]
    rows = wave_out.shape[0]
    n_time = rows * n_freq
    x0, y0 = seg // SIDE, lax.rem(seg, SIDE)
    depth = n_freq // CORES
    z0, core = freq // CORES, lax.rem(freq, CORES)

    def at(offset):
        dx, dy = offset
        return lax.rem(x0 + dx + SIDE, SIDE) * SIDE + lax.rem(y0 + dy + SIDE, SIDE)

    def along(dz, dc):
        return lax.rem(z0 + dz + depth, depth) * CORES + lax.rem(core + dc, CORES)

    plane = [at(offset) for offset in PLANE]
    n_far, n_near = 5, 4
    near, second = plane[-n_near:], plane[n_far:-n_near]
    near_line = [along(0, 1), along(1, 0), along(-1, 0)]

    barrier = pltpu.get_barrier_semaphore()
    for to in near:
        pl.semaphore_signal(barrier, 1, device_id=(freq, to), device_id_type=MESH)
    for to in near_line:
        pl.semaphore_signal(barrier, 1, device_id=(to, seg), device_id_type=MESH)

    keep = pltpu.make_async_copy(prop.at[0, seg], mats.at[seg], precv.at[seg])
    keep.start()
    begin = pltpu.make_async_copy(src.at[seg], first, fsem)
    begin.start()

    pl.semaphore_wait(barrier, len(near) + len(near_line))

    def send(to, start, length):
        cut = pl.ds(start, length)
        pltpu.make_async_remote_copy(
            prop.at[0, to, :, cut], mats.at[seg, :, cut], psend, precv.at[seg],
            device_id=(freq, to), device_id_type=MESH).start()

    def tell(devices, sem):
        for to in devices:
            pl.semaphore_signal(sem, 1, device_id=(freq, to), device_id_type=MESH)

    tell(near, plane_sem.at[0])
    for to in near:
        send(to, 0, HEAD_NEAR)
    pl.semaphore_wait(plane_sem.at[0], len(near))
    tell(second, plane_sem.at[1])
    for to in second:
        send(to, 0, HEAD_SECOND)
    pl.semaphore_wait(plane_sem.at[1], len(second))
    half = modes // 2
    for p in range(2):
        for to in plane[:n_far]:
            send(to, p * half, half)
    if HEAD_SECOND < modes:
        for to in second:
            send(to, HEAD_SECOND, modes - HEAD_SECOND)
    if HEAD_NEAR < modes:
        for to in near:
            send(to, HEAD_NEAR, modes - HEAD_NEAR)

    width = CORES * n_seg
    t = lax.broadcasted_iota(jnp.int32, (n_time, modes), 0)
    lane = lax.broadcasted_iota(jnp.int32, (n_time, modes), 1)
    column, block = lax.rem(lane, width), lane // width
    f = column // 2 + freq * n_seg
    phase = lax.rem(t * f, n_time).astype(F32) * (2.0 * np.pi / n_time)
    scale = 1.0 / np.sqrt(np.float32(n_time))
    twiddle = jnp.where(lax.rem(column, 2) == 0, jnp.cos(phase), -jnp.sin(phase)) * scale
    t_hi, t_mid, t_lo = (v.astype(F32) for v in split3(twiddle))
    zero = jnp.zeros_like(twiddle)
    table[:, :modes] = jnp.where(block < 2, t_hi, t_mid).astype(BF16)
    table[:, modes:] = jnp.where(
        block == 0, t_hi, jnp.where(block == 1, t_lo, zero)).astype(BF16)

    rounds = depth // 2
    for r in range(rounds):
        for to in near_line:
            pl.semaphore_signal(line_sem.at[r], 1, device_id=(to, seg), device_id_type=MESH)
        pl.semaphore_wait(line_sem.at[r], len(near_line))

    eye = lax.broadcasted_iota(jnp.int32, (modes, modes), 0) == lax.broadcasted_iota(
        jnp.int32, (modes, modes), 1)

    def to_row(value):
        return jnp.sum(jnp.where(eye, value, 0.0), axis=0, keepdims=True)

    def amp_copy(s):
        return pltpu.make_async_remote_copy(
            own.at[s], amp.at[seg], asend.at[s], arecv,
            device_id=(freq, s), device_id_type=MESH)

    def step(s, vec):
        re, im = vec
        pltpu.make_async_copy(mats.at[s], mats.at[s], precv.at[s]).wait()
        p_re, p_im = mats[s, 0], mats[s, 1]
        n_re = to_row(jnp.sum(p_re * re - p_im * im, axis=1, keepdims=True))
        n_im = to_row(jnp.sum(p_re * im + p_im * re, axis=1, keepdims=True))
        own[s, 0:1, :] = n_re
        own[s, 1:2, :] = n_im

        @pl.when(s == seg)
        def _():
            amp[s, 0:1, :] = n_re
            amp[s, 1:2, :] = n_im

        @pl.when(s != seg)
        def _():
            amp_copy(s).start()

        return n_re, n_im

    begin.wait()
    lax.fori_loop(0, n_seg, step, (first[0:1, :], first[1:2, :]))

    pltpu.make_async_copy(amp.at[pl.ds(0, n_seg - 1)], amp.at[pl.ds(0, n_seg - 1)], arecv).wait()
    a_hi, a_mid, a_lo = split3(amp[...].reshape(2 * n_seg, modes))
    none = jnp.zeros_like(a_hi)
    stacked = jnp.concatenate([a_hi, a_mid, a_hi, a_mid, a_lo, a_hi, none, none], axis=0)
    part[...] = jnp.dot(table[...], stacked, preferred_element_type=F32).reshape(
        n_freq, rows, modes)

    outs = []
    half = depth // 2
    for dz in sorted(range(1 - half, half + 1), key=lambda d: -abs(d)):
        for dc in range(CORES):
            if (dz, dc) == (0, 0):
                continue
            to = along(dz, dc)
            i = len(outs)
            copy = pltpu.make_async_remote_copy(
                part.at[to], got.at[i], wsend.at[i], wrecv,
                device_id=(to, seg), device_id_type=MESH)
            copy.start()
            outs.append(copy)

    amp_out[0] = amp[...]
    sent = mats.at[pl.ds(0, n_seg - 1)]
    pltpu.make_async_copy(sent, sent, psend).wait()

    def drain(s, carry):
        @pl.when(s != seg)
        def _():
            amp_copy(s).wait_send()

        return carry

    lax.fori_loop(0, n_seg, drain, 0)
    pltpu.make_async_copy(got, got, wrecv).wait()
    wave_out[:, 0, :] = part[freq] + jnp.sum(got[...], axis=0)
    for copy in outs:
        copy.wait_send()


def local(propagators, source_modes):
    n_seg, n_freq = lax.axis_size("seg"), lax.axis_size("freq")
    _, group, _, modes, _ = propagators.shape
    dma, plain = pltpu.SemaphoreType.DMA, pltpu.SemaphoreType.REGULAR
    amps, waves = pl.pallas_call(
        functools.partial(kernel, n_seg, n_freq),
        out_shape=(
            jax.ShapeDtypeStruct((1, group, 2, modes), F32),
            jax.ShapeDtypeStruct((group, 1, modes), F32),
        ),
        in_specs=[pl.BlockSpec(memory_space=pltpu.HBM)] * 2,
        out_specs=(pl.BlockSpec(memory_space=pltpu.VMEM),) * 2,
        scratch_shapes=[
            pltpu.VMEM((n_seg, 2, modes, modes), F32),
            pltpu.VMEM((n_seg, 2, modes), F32),
            pltpu.VMEM((n_seg, 2, modes), F32),
            pltpu.VMEM((n_freq, group, modes), F32),
            pltpu.VMEM((n_freq - 1, group, modes), F32),
            pltpu.VMEM((n_freq * group, 2 * modes), BF16),
            pltpu.VMEM((2, modes), F32),
            dma,
            dma((n_seg,)),
            dma((n_seg,)),
            dma,
            dma((n_freq - 1,)),
            dma,
            dma,
            plain((n_freq // CORES // 2,)),
            plain((2,)),
        ],
        compiler_params=pltpu.CompilerParams(
            collective_id=0, has_side_effects=True, vmem_limit_bytes=54500 << 10
        ),
    )(*(pltpu.with_memory_space_constraint(v, pltpu.HBM) for v in (propagators, source_modes)))

    def hand_on(a, w, a_out, w_out):
        a_out[...] = a[...]
        w_out[...] = w[...]

    return pl.pallas_call(
        hand_on,
        out_shape=(
            jax.ShapeDtypeStruct(amps.shape, F32),
            jax.ShapeDtypeStruct(waves.shape, F32),
        ),
        compiler_params=pltpu.CompilerParams(vmem_limit_bytes=4 << 20),
    )(amps, waves)


def solution(mesh):
    placed = (P("seg", "freq", None, None, None), P("freq", None, None))
    return jax.shard_map(
        local,
        mesh=mesh,
        in_specs=placed,
        out_specs=(P("seg", "freq", None, None), P("freq", "seg", None)),
        check_vma=False,
    )
```

```python
import functools

import jax
import jax.numpy as jnp
import numpy as np
from jax import lax
from jax.experimental import pallas as pl
from jax.experimental.pallas import tpu as pltpu
from jax.sharding import PartitionSpec as P

MESH = pl.DeviceIdType.MESH
F32 = jnp.float32
BF16 = jnp.bfloat16
SIDE = 4
CORES = 2
PLANE = (
    (2, 2), (1, 2), (2, 1), (-1, 2), (2, -1), (1, 1), (-1, -1), (1, -1), (-1, 1),
    (2, 0), (0, 2), (1, 0), (0, 1), (-1, 0), (0, -1),
)
HEAD_NEAR = 96
HEAD_SECOND = 64


def split3(value):
    hi = value.astype(BF16)
    rest = value - hi.astype(F32)
    mid = rest.astype(BF16)
    return hi, mid, (rest - mid.astype(F32)).astype(BF16)


def kernel(n_seg, n_freq, prop, src, amp_out, wave_out, mats, own, amp, part, got, table, first,
           psend, precv, asend, arecv, wsend, wrecv, fsem, line_sem, plane_sem):
    seg = lax.axis_index("seg")
    freq = lax.axis_index("freq")
    modes = mats.shape[-1]
    rows = wave_out.shape[0]
    n_time = rows * n_freq
    x0, y0 = seg // SIDE, lax.rem(seg, SIDE)
    depth = n_freq // CORES
    z0, core = freq // CORES, lax.rem(freq, CORES)

    def at(offset):
        dx, dy = offset
        return lax.rem(x0 + dx + SIDE, SIDE) * SIDE + lax.rem(y0 + dy + SIDE, SIDE)

    def along(dz, dc):
        return lax.rem(z0 + dz + depth, depth) * CORES + lax.rem(core + dc, CORES)

    plane = [at(offset) for offset in PLANE]
    n_far, n_near = 5, 4
    near, second = plane[-n_near:], plane[n_far:-n_near]
    near_line = [along(0, 1), along(1, 0), along(-1, 0)]

    barrier = pltpu.get_barrier_semaphore()
    for to in near:
        pl.semaphore_signal(barrier, 1, device_id=(freq, to), device_id_type=MESH)
    for to in near_line:
        pl.semaphore_signal(barrier, 1, device_id=(to, seg), device_id_type=MESH)

    keep = pltpu.make_async_copy(prop.at[0, seg], mats.at[seg], precv.at[seg])
    keep.start()
    begin = pltpu.make_async_copy(src.at[seg], first, fsem)
    begin.start()

    pl.semaphore_wait(barrier, len(near) + len(near_line))

    def send(to, start, length):
        cut = pl.ds(start, length)
        pltpu.make_async_remote_copy(
            prop.at[0, to, :, cut], mats.at[seg, :, cut], psend, precv.at[seg],
            device_id=(freq, to), device_id_type=MESH).start()

    def tell(devices, sem):
        for to in devices:
            pl.semaphore_signal(sem, 1, device_id=(freq, to), device_id_type=MESH)

    tell(near, plane_sem.at[0])
    for to in near:
        send(to, 0, HEAD_NEAR)
    pl.semaphore_wait(plane_sem.at[0], len(near))
    tell(second, plane_sem.at[1])
    for to in second:
        send(to, 0, HEAD_SECOND)
    pl.semaphore_wait(plane_sem.at[1], len(second))
    half = modes // 2
    for p in range(2):
        for to in plane[:n_far]:
            send(to, p * half, half)
    if HEAD_SECOND < modes:
        for to in second:
            send(to, HEAD_SECOND, modes - HEAD_SECOND)
    if HEAD_NEAR < modes:
        for to in near:
            send(to, HEAD_NEAR, modes - HEAD_NEAR)

    width = CORES * n_seg
    t = lax.broadcasted_iota(jnp.int32, (n_time, modes), 0)
    lane = lax.broadcasted_iota(jnp.int32, (n_time, modes), 1)
    column, block = lax.rem(lane, width), lane // width
    f = column // 2 + freq * n_seg
    phase = lax.rem(t * f, n_time).astype(F32) * (2.0 * np.pi / n_time)
    scale = 1.0 / np.sqrt(np.float32(n_time))
    twiddle = jnp.where(lax.rem(column, 2) == 0, jnp.cos(phase), -jnp.sin(phase)) * scale
    t_hi, t_mid, t_lo = (v.astype(F32) for v in split3(twiddle))
    zero = jnp.zeros_like(twiddle)
    table[:, :modes] = jnp.where(block < 2, t_hi, t_mid).astype(BF16)
    table[:, modes:] = jnp.where(
        block == 0, t_hi, jnp.where(block == 1, t_lo, zero)).astype(BF16)

    rounds = depth // 2
    for r in range(rounds):
        for to in near_line:
            pl.semaphore_signal(line_sem.at[r], 1, device_id=(to, seg), device_id_type=MESH)
        pl.semaphore_wait(line_sem.at[r], len(near_line))

    eye = lax.broadcasted_iota(jnp.int32, (modes, modes), 0) == lax.broadcasted_iota(
        jnp.int32, (modes, modes), 1)

    def to_row(value):
        return jnp.sum(jnp.where(eye, value, 0.0), axis=0, keepdims=True)

    def amp_copy(s):
        return pltpu.make_async_remote_copy(
            own.at[s], amp.at[seg], asend.at[s], arecv,
            device_id=(freq, s), device_id_type=MESH)

    def fetch(s):
        pltpu.make_async_copy(mats.at[s], mats.at[s], precv.at[s]).wait()
        return mats[s, 0], mats[s, 1]

    def give(s, re, im):
        own[s, 0:1, :] = re
        own[s, 1:2, :] = im

        @pl.when(s == seg)
        def _():
            amp[s, 0:1, :] = re
            amp[s, 1:2, :] = im

        @pl.when(s != seg)
        def _():
            amp_copy(s).start()

    def step(k, vec):
        re, im = vec
        p_re, p_im = fetch(2 * k)
        c_re = jnp.sum(p_re * re - p_im * im, axis=1, keepdims=True)
        c_im = jnp.sum(p_re * im + p_im * re, axis=1, keepdims=True)
        give(2 * k, to_row(c_re), to_row(c_im))
        q_re, q_im = (v.T for v in fetch(2 * k + 1))
        re = jnp.sum(q_re * c_re - q_im * c_im, axis=0, keepdims=True)
        im = jnp.sum(q_re * c_im + q_im * c_re, axis=0, keepdims=True)
        give(2 * k + 1, re, im)
        return re, im

    begin.wait()
    lax.fori_loop(0, n_seg // 2, step, (first[0:1, :], first[1:2, :]))

    pltpu.make_async_copy(amp.at[pl.ds(0, n_seg - 1)], amp.at[pl.ds(0, n_seg - 1)], arecv).wait()
    a_hi, a_mid, a_lo = split3(amp[...].reshape(2 * n_seg, modes))
    none = jnp.zeros_like(a_hi)
    stacked = jnp.concatenate([a_hi, a_mid, a_hi, a_mid, a_lo, a_hi, none, none], axis=0)
    part[...] = jnp.dot(table[...], stacked, preferred_element_type=F32).reshape(
        n_freq, rows, modes)

    outs = []
    half = depth // 2
    for dz in sorted(range(1 - half, half + 1), key=lambda d: -abs(d)):
        for dc in range(CORES):
            if (dz, dc) == (0, 0):
                continue
            to = along(dz, dc)
            i = len(outs)
            copy = pltpu.make_async_remote_copy(
                part.at[to], got.at[i], wsend.at[i], wrecv,
                device_id=(to, seg), device_id_type=MESH)
            copy.start()
            outs.append(copy)

    amp_out[0] = amp[...]
    sent = mats.at[pl.ds(0, n_seg - 1)]
    pltpu.make_async_copy(sent, sent, psend).wait()

    def drain(s, carry):
        @pl.when(s != seg)
        def _():
            amp_copy(s).wait_send()

        return carry

    lax.fori_loop(0, n_seg, drain, 0)
    pltpu.make_async_copy(got, got, wrecv).wait()
    wave_out[:, 0, :] = part[freq] + jnp.sum(got[...], axis=0)
    for copy in outs:
        copy.wait_send()


def local(propagators, source_modes):
    n_seg, n_freq = lax.axis_size("seg"), lax.axis_size("freq")
    _, group, _, modes, _ = propagators.shape
    dma, plain = pltpu.SemaphoreType.DMA, pltpu.SemaphoreType.REGULAR
    amps, waves = pl.pallas_call(
        functools.partial(kernel, n_seg, n_freq),
        out_shape=(
            jax.ShapeDtypeStruct((1, group, 2, modes), F32),
            jax.ShapeDtypeStruct((group, 1, modes), F32),
        ),
        in_specs=[pl.BlockSpec(memory_space=pltpu.HBM)] * 2,
        out_specs=(pl.BlockSpec(memory_space=pltpu.VMEM),) * 2,
        scratch_shapes=[
            pltpu.VMEM((n_seg, 2, modes, modes), F32),
            pltpu.VMEM((n_seg, 2, modes), F32),
            pltpu.VMEM((n_seg, 2, modes), F32),
            pltpu.VMEM((n_freq, group, modes), F32),
            pltpu.VMEM((n_freq - 1, group, modes), F32),
            pltpu.VMEM((n_freq * group, 2 * modes), BF16),
            pltpu.VMEM((2, modes), F32),
            dma,
            dma((n_seg,)),
            dma((n_seg,)),
            dma,
            dma((n_freq - 1,)),
            dma,
            dma,
            plain((n_freq // CORES // 2,)),
            plain((2,)),
        ],
        compiler_params=pltpu.CompilerParams(
            collective_id=0, has_side_effects=True, vmem_limit_bytes=54500 << 10
        ),
    )(*(pltpu.with_memory_space_constraint(v, pltpu.HBM) for v in (propagators, source_modes)))

    def hand_on(a, w, a_out, w_out):
        a_out[...] = a[...]
        w_out[...] = w[...]

    return pl.pallas_call(
        hand_on,
        out_shape=(
            jax.ShapeDtypeStruct(amps.shape, F32),
            jax.ShapeDtypeStruct(waves.shape, F32),
        ),
        compiler_params=pltpu.CompilerParams(vmem_limit_bytes=4 << 20),
    )(amps, waves)


def solution(mesh):
    placed = (P("seg", "freq", None, None, None), P("freq", None, None))
    return jax.shard_map(
        local,
        mesh=mesh,
        in_specs=placed,
        out_specs=(P("seg", "freq", None, None), P("freq", "seg", None)),
        check_vma=False,
    )
```

```python
import functools

import jax
import jax.numpy as jnp
import numpy as np
from jax import lax
from jax.experimental import pallas as pl
from jax.experimental.pallas import tpu as pltpu
from jax.sharding import PartitionSpec as P

MESH = pl.DeviceIdType.MESH
F32 = jnp.float32
BF16 = jnp.bfloat16
SIDE = 4
CORES = 2
PLANE = (
    (2, 2), (1, 2), (2, 1), (-1, 2), (2, -1), (1, 1), (-1, -1), (1, -1), (-1, 1),
    (2, 0), (0, 2), (1, 0), (0, 1), (-1, 0), (0, -1),
)
DIRECT = 48
HEAD_NEAR = 96
HEAD_SECOND = 64


def split3(value):
    hi = value.astype(BF16)
    rest = value - hi.astype(F32)
    mid = rest.astype(BF16)
    return hi, mid, (rest - mid.astype(F32)).astype(BF16)


def kernel(n_seg, n_freq, prop, src, amp_out, wave_out, mats, own, amp, part, got, table, first,
           psend, precv, asend, arecv, wsend, wrecv, fsem, line_sem, plane_sem, relay,
           relay_send, relay_recv, hello, ask, go):
    seg = lax.axis_index("seg")
    freq = lax.axis_index("freq")
    modes = mats.shape[-1]
    rows = wave_out.shape[0]
    n_time = rows * n_freq
    x0, y0 = seg // SIDE, lax.rem(seg, SIDE)
    depth = n_freq // CORES
    z0, core = freq // CORES, lax.rem(freq, CORES)

    def at(offset):
        dx, dy = offset
        return lax.rem(x0 + dx + SIDE, SIDE) * SIDE + lax.rem(y0 + dy + SIDE, SIDE)

    def along(dz, dc):
        return lax.rem(z0 + dz + depth, depth) * CORES + lax.rem(core + dc, CORES)

    plane = [at(offset) for offset in PLANE]
    n_far, n_near = 5, 4
    near, second = plane[-n_near:], plane[n_far:-n_near]
    near_line = [along(0, 1), along(1, 0), along(-1, 0)]
    middle = depth // 2
    late = z0 >= middle
    helps = z0 < middle - 1
    helps_two = z0 == 0
    slot = jnp.where(z0 == middle, 1, 0)
    helper = jnp.where(z0 == middle, 0, depth - 1 - z0) * CORES + core
    clients = ((depth - 1 - z0) * CORES + core, middle * CORES + core)

    barrier = pltpu.get_barrier_semaphore()

    def greet(line, plane_to):
        pl.semaphore_signal(barrier, 1, device_id=(line, plane_to), device_id_type=MESH)

    for to in near:
        greet(freq, to)
    greet(along(0, 1), seg)

    @pl.when(z0 < depth - 1)
    def _():
        greet(along(1, 0), seg)

    @pl.when(helps)
    def _():
        greet(clients[0], seg)

    @pl.when(helps_two)
    def _():
        greet(clients[1], seg)

    keep = pltpu.make_async_copy(prop.at[0, seg], mats.at[seg], precv.at[seg])
    keep.start()
    begin = pltpu.make_async_copy(src.at[seg], first, fsem)
    begin.start()

    below = jnp.where(z0 > 0, 1, 0)
    is_late = jnp.where(late, 1, 0)
    pl.semaphore_wait(barrier, len(near) + 1 + below + is_late)

    def send(to, start, length):
        cut = pl.ds(start, length)
        pltpu.make_async_remote_copy(
            prop.at[0, to, :, cut], mats.at[seg, :, cut], psend, precv.at[seg],
            device_id=(freq, to), device_id_type=MESH).start()

    def tell(devices, sem):
        for to in devices:
            pl.semaphore_signal(sem, 1, device_id=(freq, to), device_id_type=MESH)

    def send_farthest(p, length):
        @pl.when(jnp.logical_not(late))
        def _():
            send(plane[0], p * length, length)

        if DIRECT > p * length:
            @pl.when(late)
            def _():
                send(plane[0], p * length, min(length, DIRECT - p * length))

    def send_relayed():
        @pl.when(late)
        def _():
            pl.semaphore_wait(go, 1)
            cut = pl.ds(DIRECT, modes - DIRECT)
            pltpu.make_async_remote_copy(
                prop.at[0, plane[0], :, cut], relay.at[slot], psend, relay_recv.at[slot],
                device_id=(helper, plane[0]), device_id_type=MESH).start()

    tell(near, plane_sem.at[0])
    for to in near:
        send(to, 0, HEAD_NEAR)
    @pl.when(z0 > 0)
    def _():
        pl.semaphore_signal(hello, 1, device_id=(along(-1, 0), seg), device_id_type=MESH)

    @pl.when(late)
    def _():
        pl.semaphore_signal(ask, 1, device_id=(helper, seg), device_id_type=MESH)

    @pl.when(z0 == depth - 1)
    def _():
        pl.semaphore_signal(hello, 1, device_id=(along(1, 0), seg), device_id_type=MESH)


    pl.semaphore_wait(plane_sem.at[0], len(near))
    tell(second, plane_sem.at[1])
    for to in second:
        send(to, 0, HEAD_SECOND)
    pl.semaphore_wait(plane_sem.at[1], len(second))
    half = modes // 2
    for p in range(2):
        send_farthest(p, half)
        for to in plane[1:n_far]:
            send(to, p * half, half)
        if p == 0:
            send_relayed()
    if HEAD_SECOND < modes:
        for to in second:
            send(to, HEAD_SECOND, modes - HEAD_SECOND)
    if HEAD_NEAR < modes:
        for to in near:
            send(to, HEAD_NEAR, modes - HEAD_NEAR)

    forward = [
        pltpu.make_async_remote_copy(
            relay.at[i], mats.at[plane[0], :, pl.ds(DIRECT, modes - DIRECT)], relay_send.at[i],
            precv.at[plane[0]], device_id=(client, seg), device_id_type=MESH)
        for i, client in enumerate(clients)
    ]

    @pl.when(helps_two)
    def _():
        pl.semaphore_wait(ask, 2)
        for client in clients:
            pl.semaphore_signal(go, 1, device_id=(client, seg), device_id_type=MESH)

    @pl.when(jnp.logical_and(helps, jnp.logical_not(helps_two)))
    def _():
        pl.semaphore_wait(ask, 1)
        pl.semaphore_signal(go, 1, device_id=(clients[0], seg), device_id_type=MESH)

    width = CORES * n_seg
    t = lax.broadcasted_iota(jnp.int32, (n_time, modes), 0)
    lane = lax.broadcasted_iota(jnp.int32, (n_time, modes), 1)
    column, block = lax.rem(lane, width), lane // width
    f = column // 2 + freq * n_seg
    phase = lax.rem(t * f, n_time).astype(F32) * (2.0 * np.pi / n_time)
    scale = 1.0 / np.sqrt(np.float32(n_time))
    twiddle = jnp.where(lax.rem(column, 2) == 0, jnp.cos(phase), -jnp.sin(phase)) * scale
    t_hi, t_mid, t_lo = (v.astype(F32) for v in split3(twiddle))
    zero = jnp.zeros_like(twiddle)
    table[:, :modes] = jnp.where(block < 2, t_hi, t_mid).astype(BF16)
    table[:, modes:] = jnp.where(
        block == 0, t_hi, jnp.where(block == 1, t_lo, zero)).astype(BF16)

    for i, here in enumerate((helps, helps_two)):
        @pl.when(here)
        def _(i=i):
            pltpu.make_async_copy(relay.at[i], relay.at[i], relay_recv.at[i]).wait()
            forward[i].start()

    @pl.when(z0 == 0)
    def _():
        pl.semaphore_wait(hello, 2)

    @pl.when(jnp.logical_and(z0 > 0, z0 < depth - 1))
    def _():
        pl.semaphore_wait(hello, 1)

    rounds = depth // 2
    for r in range(rounds):
        for to in near_line:
            pl.semaphore_signal(line_sem.at[r], 1, device_id=(to, seg), device_id_type=MESH)
        pl.semaphore_wait(line_sem.at[r], len(near_line))

    eye = lax.broadcasted_iota(jnp.int32, (modes, modes), 0) == lax.broadcasted_iota(
        jnp.int32, (modes, modes), 1)

    def to_row(value):
        return jnp.sum(jnp.where(eye, value, 0.0), axis=0, keepdims=True)

    def amp_copy(s):
        return pltpu.make_async_remote_copy(
            own.at[s], amp.at[seg], asend.at[s], arecv,
            device_id=(freq, s), device_id_type=MESH)

    def fetch(s):
        pltpu.make_async_copy(mats.at[s], mats.at[s], precv.at[s]).wait()
        return mats[s, 0], mats[s, 1]

    def give(s, re, im):
        own[s, 0:1, :] = re
        own[s, 1:2, :] = im

        @pl.when(s == seg)
        def _():
            amp[s, 0:1, :] = re
            amp[s, 1:2, :] = im

        @pl.when(s != seg)
        def _():
            amp_copy(s).start()

    def step(k, vec):
        re, im = vec
        p_re, p_im = fetch(2 * k)
        c_re = jnp.sum(p_re * re - p_im * im, axis=1, keepdims=True)
        c_im = jnp.sum(p_re * im + p_im * re, axis=1, keepdims=True)
        give(2 * k, to_row(c_re), to_row(c_im))
        q_re, q_im = (v.T for v in fetch(2 * k + 1))
        re = jnp.sum(q_re * c_re - q_im * c_im, axis=0, keepdims=True)
        im = jnp.sum(q_re * c_im + q_im * c_re, axis=0, keepdims=True)
        give(2 * k + 1, re, im)
        return re, im

    begin.wait()
    lax.fori_loop(0, n_seg // 2, step, (first[0:1, :], first[1:2, :]))

    pltpu.make_async_copy(amp.at[pl.ds(0, n_seg - 1)], amp.at[pl.ds(0, n_seg - 1)], arecv).wait()
    a_hi, a_mid, a_lo = split3(amp[...].reshape(2 * n_seg, modes))
    none = jnp.zeros_like(a_hi)
    stacked = jnp.concatenate([a_hi, a_mid, a_hi, a_mid, a_lo, a_hi, none, none], axis=0)
    part[...] = jnp.dot(table[...], stacked, preferred_element_type=F32).reshape(
        n_freq, rows, modes)

    outs = []
    half = depth // 2
    for dz in sorted(range(1 - half, half + 1), key=lambda d: -abs(d)):
        for dc in range(CORES):
            if (dz, dc) == (0, 0):
                continue
            to = along(dz, dc)
            i = len(outs)
            copy = pltpu.make_async_remote_copy(
                part.at[to], got.at[i], wsend.at[i], wrecv,
                device_id=(to, seg), device_id_type=MESH)
            copy.start()
            outs.append(copy)

    amp_out[0] = amp[...]
    sent = mats.at[pl.ds(0, n_seg - 1)]
    pltpu.make_async_copy(sent, sent, psend).wait()

    def drain(s, carry):
        @pl.when(s != seg)
        def _():
            amp_copy(s).wait_send()

        return carry

    lax.fori_loop(0, n_seg, drain, 0)
    pltpu.make_async_copy(got, got, wrecv).wait()
    wave_out[:, 0, :] = part[freq] + jnp.sum(got[...], axis=0)
    for copy in outs:
        copy.wait_send()

    for i, here in enumerate((helps, helps_two)):
        @pl.when(here)
        def _(i=i):
            forward[i].wait_send()


def local(propagators, source_modes):
    n_seg, n_freq = lax.axis_size("seg"), lax.axis_size("freq")
    _, group, _, modes, _ = propagators.shape
    dma, plain = pltpu.SemaphoreType.DMA, pltpu.SemaphoreType.REGULAR
    amps, waves = pl.pallas_call(
        functools.partial(kernel, n_seg, n_freq),
        out_shape=(
            jax.ShapeDtypeStruct((1, group, 2, modes), F32),
            jax.ShapeDtypeStruct((group, 1, modes), F32),
        ),
        in_specs=[pl.BlockSpec(memory_space=pltpu.HBM)] * 2,
        out_specs=(pl.BlockSpec(memory_space=pltpu.VMEM),) * 2,
        scratch_shapes=[
            pltpu.VMEM((n_seg, 2, modes, modes), F32),
            pltpu.VMEM((n_seg, 2, modes), F32),
            pltpu.VMEM((n_seg, 2, modes), F32),
            pltpu.VMEM((n_freq, group, modes), F32),
            pltpu.VMEM((n_freq - 1, group, modes), F32),
            pltpu.VMEM((n_freq * group, 2 * modes), BF16),
            pltpu.VMEM((2, modes), F32),
            dma,
            dma((n_seg,)),
            dma((n_seg,)),
            dma,
            dma((n_freq - 1,)),
            dma,
            dma,
            plain((n_freq // CORES // 2,)),
            plain((2,)),
            pltpu.VMEM((2, 2, modes - DIRECT, modes), F32),
            dma((2,)),
            dma((2,)),
            plain,
            plain,
            plain,
        ],
        compiler_params=pltpu.CompilerParams(
            collective_id=0, has_side_effects=True, vmem_limit_bytes=54500 << 10
        ),
    )(*(pltpu.with_memory_space_constraint(v, pltpu.HBM) for v in (propagators, source_modes)))

    def hand_on(a, w, a_out, w_out):
        a_out[...] = a[...]
        w_out[...] = w[...]

    return pl.pallas_call(
        hand_on,
        out_shape=(
            jax.ShapeDtypeStruct(amps.shape, F32),
            jax.ShapeDtypeStruct(waves.shape, F32),
        ),
        compiler_params=pltpu.CompilerParams(vmem_limit_bytes=4 << 20),
    )(amps, waves)


def solution(mesh):
    placed = (P("seg", "freq", None, None, None), P("freq", None, None))
    return jax.shard_map(
        local,
        mesh=mesh,
        in_specs=placed,
        out_specs=(P("seg", "freq", None, None), P("freq", "seg", None)),
        check_vma=False,
    )
```

```python
import functools

import jax
import jax.numpy as jnp
import numpy as np
from jax import lax
from jax.experimental import pallas as pl
from jax.experimental.pallas import tpu as pltpu
from jax.sharding import PartitionSpec as P

MESH = pl.DeviceIdType.MESH
F32 = jnp.float32
BF16 = jnp.bfloat16
SIDE = 4
CORES = 2
PLANE = (
    (2, 2), (1, 2), (2, 1), (-1, 2), (2, -1), (1, 1), (-1, -1), (1, -1), (-1, 1),
    (2, 0), (0, 2), (1, 0), (0, 1), (-1, 0), (0, -1),
)
DIRECT = 48
HEAD_NEAR = 96
HEAD_SECOND = 64


def split3(value):
    hi = value.astype(BF16)
    rest = value - hi.astype(F32)
    mid = rest.astype(BF16)
    return hi, mid, (rest - mid.astype(F32)).astype(BF16)


def kernel(n_seg, n_freq, prop, src, amp_out, wave_out, mats, own, amp, part, got, table, first,
           psend, precv, asend, arecv, wsend, wrecv, fsem, line_sem, plane_sem, relay,
           relay_send, relay_recv, hello, ask, go):
    seg = lax.axis_index("seg")
    freq = lax.axis_index("freq")
    modes = mats.shape[-1]
    rows = wave_out.shape[0]
    n_time = rows * n_freq
    x0, y0 = lax.div(seg, SIDE), lax.rem(seg, SIDE)
    depth = n_freq // CORES
    z0, core = lax.div(freq, CORES), lax.rem(freq, CORES)
    across = {d: lax.rem(x0 + d + SIDE, SIDE) * SIDE for d in (1, -1, 2)} | {0: x0 * SIDE}
    down = {d: lax.rem(y0 + d + SIDE, SIDE) for d in (1, -1, 2)} | {0: y0}

    def at(offset):
        dx, dy = offset
        return across[dx] + down[dy]

    def along(dz, dc):
        return lax.rem(z0 + dz + depth, depth) * CORES + lax.rem(core + dc, CORES)

    plane = [at(offset) for offset in PLANE]
    n_far, n_near = 5, 4
    near, second = plane[-n_near:], plane[n_far:-n_near]
    near_line = [along(0, 1), along(1, 0), along(-1, 0)]
    middle = depth // 2
    late = z0 >= middle
    helps = z0 < middle - 1
    helps_two = z0 == 0
    slot = jnp.where(z0 == middle, 1, 0)
    helper = jnp.where(z0 == middle, 0, depth - 1 - z0) * CORES + core
    clients = ((depth - 1 - z0) * CORES + core, middle * CORES + core)

    barrier = pltpu.get_barrier_semaphore()

    def greet(line, plane_to):
        pl.semaphore_signal(barrier, 1, device_id=(line, plane_to), device_id_type=MESH)

    for to in near:
        greet(freq, to)
    greet(along(0, 1), seg)

    @pl.when(z0 < depth - 1)
    def _():
        greet(along(1, 0), seg)

    @pl.when(helps)
    def _():
        greet(clients[0], seg)

    @pl.when(helps_two)
    def _():
        greet(clients[1], seg)

    keep = pltpu.make_async_copy(prop.at[0, seg], mats.at[seg], precv.at[seg])
    keep.start()
    begin = pltpu.make_async_copy(src.at[seg], first, fsem)
    begin.start()

    below = jnp.where(z0 > 0, 1, 0)
    is_late = jnp.where(late, 1, 0)
    pl.semaphore_wait(barrier, len(near) + 1 + below + is_late)

    def send(to, start, length):
        cut = pl.ds(start, length)
        pltpu.make_async_remote_copy(
            prop.at[0, to, :, cut], mats.at[seg, :, cut], psend, precv.at[seg],
            device_id=(freq, to), device_id_type=MESH).start()

    def tell(devices, sem):
        for to in devices:
            pl.semaphore_signal(sem, 1, device_id=(freq, to), device_id_type=MESH)

    def send_farthest(p, length):
        @pl.when(jnp.logical_not(late))
        def _():
            send(plane[0], p * length, length)

        if DIRECT > p * length:
            @pl.when(late)
            def _():
                send(plane[0], p * length, min(length, DIRECT - p * length))

    def send_relayed():
        @pl.when(late)
        def _():
            pl.semaphore_wait(go, 1)
            cut = pl.ds(DIRECT, modes - DIRECT)
            pltpu.make_async_remote_copy(
                prop.at[0, plane[0], :, cut], relay.at[slot], psend, relay_recv.at[slot],
                device_id=(helper, plane[0]), device_id_type=MESH).start()

    tell(near, plane_sem.at[0])
    for to in near:
        send(to, 0, HEAD_NEAR)
    @pl.when(z0 > 0)
    def _():
        pl.semaphore_signal(hello, 1, device_id=(along(-1, 0), seg), device_id_type=MESH)

    @pl.when(late)
    def _():
        pl.semaphore_signal(ask, 1, device_id=(helper, seg), device_id_type=MESH)

    @pl.when(z0 == depth - 1)
    def _():
        pl.semaphore_signal(hello, 1, device_id=(along(1, 0), seg), device_id_type=MESH)


    pl.semaphore_wait(plane_sem.at[0], len(near))
    tell(second, plane_sem.at[1])
    for to in second:
        send(to, 0, HEAD_SECOND)
    pl.semaphore_wait(plane_sem.at[1], len(second))
    half = modes // 2
    for p in range(2):
        send_farthest(p, half)
        for to in plane[1:n_far]:
            send(to, p * half, half)
        if p == 0:
            send_relayed()
    if HEAD_SECOND < modes:
        for to in second:
            send(to, HEAD_SECOND, modes - HEAD_SECOND)
    if HEAD_NEAR < modes:
        for to in near:
            send(to, HEAD_NEAR, modes - HEAD_NEAR)

    forward = [
        pltpu.make_async_remote_copy(
            relay.at[i], mats.at[plane[0], :, pl.ds(DIRECT, modes - DIRECT)], relay_send.at[i],
            precv.at[plane[0]], device_id=(client, seg), device_id_type=MESH)
        for i, client in enumerate(clients)
    ]

    @pl.when(helps_two)
    def _():
        pl.semaphore_wait(ask, 2)
        for client in clients:
            pl.semaphore_signal(go, 1, device_id=(client, seg), device_id_type=MESH)

    @pl.when(jnp.logical_and(helps, jnp.logical_not(helps_two)))
    def _():
        pl.semaphore_wait(ask, 1)
        pl.semaphore_signal(go, 1, device_id=(clients[0], seg), device_id_type=MESH)

    width = CORES * n_seg
    t = lax.broadcasted_iota(jnp.int32, (n_time, modes), 0)
    lane = lax.broadcasted_iota(jnp.int32, (n_time, modes), 1)
    column, block = lax.rem(lane, width), lane // width
    f = column // 2 + freq * n_seg
    phase = lax.rem(t * f, n_time).astype(F32) * (2.0 * np.pi / n_time)
    scale = 1.0 / np.sqrt(np.float32(n_time))
    twiddle = jnp.where(lax.rem(column, 2) == 0, jnp.cos(phase), -jnp.sin(phase)) * scale
    t_hi, t_mid, t_lo = (v.astype(F32) for v in split3(twiddle))
    zero = jnp.zeros_like(twiddle)
    table[:, :modes] = jnp.where(block < 2, t_hi, t_mid).astype(BF16)
    table[:, modes:] = jnp.where(
        block == 0, t_hi, jnp.where(block == 1, t_lo, zero)).astype(BF16)

    for i, here in enumerate((helps, helps_two)):
        @pl.when(here)
        def _(i=i):
            pltpu.make_async_copy(relay.at[i], relay.at[i], relay_recv.at[i]).wait()
            forward[i].start()

    @pl.when(z0 == 0)
    def _():
        pl.semaphore_wait(hello, 2)

    @pl.when(jnp.logical_and(z0 > 0, z0 < depth - 1))
    def _():
        pl.semaphore_wait(hello, 1)

    rounds = depth // 2
    for r in range(rounds):
        for to in near_line:
            pl.semaphore_signal(line_sem.at[r], 1, device_id=(to, seg), device_id_type=MESH)
        pl.semaphore_wait(line_sem.at[r], len(near_line))

    eye = lax.broadcasted_iota(jnp.int32, (modes, modes), 0) == lax.broadcasted_iota(
        jnp.int32, (modes, modes), 1)

    def to_row(value):
        return jnp.sum(jnp.where(eye, value, 0.0), axis=0, keepdims=True)

    def amp_copy(s):
        return pltpu.make_async_remote_copy(
            own.at[s], amp.at[seg], asend.at[s], arecv,
            device_id=(freq, s), device_id_type=MESH)

    def fetch(s):
        pltpu.make_async_copy(mats.at[s], mats.at[s], precv.at[s]).wait()
        return mats[s, 0], mats[s, 1]

    def give(s, re, im):
        own[s, 0:1, :] = re
        own[s, 1:2, :] = im

        @pl.when(s != seg)
        def _():
            amp_copy(s).start()

    def step(k, vec):
        re, im = vec
        p_re, p_im = fetch(2 * k)
        c_re = jnp.sum(p_re * re - p_im * im, axis=1, keepdims=True)
        c_im = jnp.sum(p_re * im + p_im * re, axis=1, keepdims=True)
        give(2 * k, to_row(c_re), to_row(c_im))
        q_re, q_im = (v.T for v in fetch(2 * k + 1))
        re = jnp.sum(q_re * c_re - q_im * c_im, axis=0, keepdims=True)
        im = jnp.sum(q_re * c_im + q_im * c_re, axis=0, keepdims=True)
        give(2 * k + 1, re, im)
        return re, im

    begin.wait()
    lax.fori_loop(0, n_seg // 2, step, (first[0:1, :], first[1:2, :]))
    amp[seg] = own[seg]

    pltpu.make_async_copy(amp.at[pl.ds(0, n_seg - 1)], amp.at[pl.ds(0, n_seg - 1)], arecv).wait()
    a_hi, a_mid, a_lo = split3(amp[...].reshape(2 * n_seg, modes))
    none = jnp.zeros_like(a_hi)
    stacked = jnp.concatenate([a_hi, a_mid, a_hi, a_mid, a_lo, a_hi, none, none], axis=0)
    part[...] = jnp.dot(table[...], stacked, preferred_element_type=F32).reshape(
        n_freq, rows, modes)

    outs = []
    half = depth // 2
    for dz in sorted(range(1 - half, half + 1), key=lambda d: -abs(d)):
        for dc in range(CORES):
            if (dz, dc) == (0, 0):
                continue
            to = along(dz, dc)
            i = len(outs)
            copy = pltpu.make_async_remote_copy(
                part.at[to], got.at[i], wsend.at[i], wrecv,
                device_id=(to, seg), device_id_type=MESH)
            copy.start()
            outs.append(copy)

    amp_out[0] = amp[...]
    sent = mats.at[pl.ds(0, n_seg - 1)]
    pltpu.make_async_copy(sent, sent, psend).wait()

    def drain(s, carry):
        @pl.when(s != seg)
        def _():
            amp_copy(s).wait_send()

        return carry

    lax.fori_loop(0, n_seg, drain, 0)
    pltpu.make_async_copy(got, got, wrecv).wait()
    wave_out[:, 0, :] = part[freq] + jnp.sum(got[...], axis=0)
    for copy in outs:
        copy.wait_send()

    for i, here in enumerate((helps, helps_two)):
        @pl.when(here)
        def _(i=i):
            forward[i].wait_send()


def local(propagators, source_modes):
    n_seg, n_freq = lax.axis_size("seg"), lax.axis_size("freq")
    _, group, _, modes, _ = propagators.shape
    dma, plain = pltpu.SemaphoreType.DMA, pltpu.SemaphoreType.REGULAR
    amps, waves = pl.pallas_call(
        functools.partial(kernel, n_seg, n_freq),
        out_shape=(
            jax.ShapeDtypeStruct((1, group, 2, modes), F32),
            jax.ShapeDtypeStruct((group, 1, modes), F32),
        ),
        in_specs=[pl.BlockSpec(memory_space=pltpu.HBM)] * 2,
        out_specs=(pl.BlockSpec(memory_space=pltpu.VMEM),) * 2,
        scratch_shapes=[
            pltpu.VMEM((n_seg, 2, modes, modes), F32),
            pltpu.VMEM((n_seg, 2, modes), F32),
            pltpu.VMEM((n_seg, 2, modes), F32),
            pltpu.VMEM((n_freq, group, modes), F32),
            pltpu.VMEM((n_freq - 1, group, modes), F32),
            pltpu.VMEM((n_freq * group, 2 * modes), BF16),
            pltpu.VMEM((2, modes), F32),
            dma,
            dma((n_seg,)),
            dma((n_seg,)),
            dma,
            dma((n_freq - 1,)),
            dma,
            dma,
            plain((n_freq // CORES // 2,)),
            plain((2,)),
            pltpu.VMEM((2, 2, modes - DIRECT, modes), F32),
            dma((2,)),
            dma((2,)),
            plain,
            plain,
            plain,
        ],
        compiler_params=pltpu.CompilerParams(
            collective_id=0, has_side_effects=True, vmem_limit_bytes=54500 << 10
        ),
    )(*(pltpu.with_memory_space_constraint(v, pltpu.HBM) for v in (propagators, source_modes)))

    def hand_on(a, w, a_out, w_out):
        a_out[...] = a[...]
        w_out[...] = w[...]

    return pl.pallas_call(
        hand_on,
        out_shape=(
            jax.ShapeDtypeStruct(amps.shape, F32),
            jax.ShapeDtypeStruct(waves.shape, F32),
        ),
        compiler_params=pltpu.CompilerParams(vmem_limit_bytes=4 << 20),
    )(amps, waves)


def solution(mesh):
    placed = (P("seg", "freq", None, None, None), P("freq", None, None))
    return jax.shard_map(
        local,
        mesh=mesh,
        in_specs=placed,
        out_specs=(P("seg", "freq", None, None), P("freq", "seg", None)),
        check_vma=False,
    )
```

```python
import functools

import jax
import jax.numpy as jnp
import numpy as np
from jax import lax
from jax.experimental import pallas as pl
from jax.experimental.pallas import tpu as pltpu
from jax.sharding import PartitionSpec as P

MESH = pl.DeviceIdType.MESH
F32 = jnp.float32
BF16 = jnp.bfloat16
SIDE = 4
CORES = 2
PLANE = (
    (2, 2), (1, 2), (2, 1), (-1, 2), (2, -1), (1, 1), (-1, -1), (1, -1), (-1, 1),
    (2, 0), (0, 2), (1, 0), (0, 1), (-1, 0), (0, -1),
)
DIRECT = 48
HEAD_NEAR = 96
HEAD_SECOND = 64


def split3(value):
    hi = value.astype(BF16)
    rest = value - hi.astype(F32)
    mid = rest.astype(BF16)
    return hi, mid, (rest - mid.astype(F32)).astype(BF16)


def kernel(n_seg, n_freq, prop, src, amp_out, wave_out, mats, own, amp, part, got, table, first,
           psend, precv, asend, arecv, wsend, wrecv, fsem, line_sem, plane_sem, relay,
           relay_send, relay_recv, hello, ask, go):
    seg = lax.axis_index("seg")
    freq = lax.axis_index("freq")
    modes = mats.shape[-1]
    rows = wave_out.shape[0]
    n_time = rows * n_freq
    x0, y0 = lax.div(seg, SIDE), lax.rem(seg, SIDE)
    depth = n_freq // CORES
    z0, core = lax.div(freq, CORES), lax.rem(freq, CORES)
    across = {d: lax.rem(x0 + d + SIDE, SIDE) * SIDE for d in (1, -1, 2)} | {0: x0 * SIDE}
    down = {d: lax.rem(y0 + d + SIDE, SIDE) for d in (1, -1, 2)} | {0: y0}

    def at(offset):
        dx, dy = offset
        return across[dx] + down[dy]

    def along(dz, dc):
        return lax.rem(z0 + dz + depth, depth) * CORES + lax.rem(core + dc, CORES)

    plane = [at(offset) for offset in PLANE]
    n_far, n_near = 5, 4
    near, second = plane[-n_near:], plane[n_far:-n_near]
    near_line = [along(0, 1), along(1, 0), along(-1, 0)]
    middle = depth // 2
    late = z0 >= middle
    helps = z0 < middle - 1
    helps_two = z0 == 0
    slot = jnp.where(z0 == middle, 1, 0)
    helper = jnp.where(z0 == middle, 0, depth - 1 - z0) * CORES + core
    clients = ((depth - 1 - z0) * CORES + core, middle * CORES + core)

    barrier = pltpu.get_barrier_semaphore()

    def greet(line, plane_to):
        pl.semaphore_signal(barrier, 1, device_id=(line, plane_to), device_id_type=MESH)

    for to in near:
        greet(freq, to)
    greet(along(0, 1), seg)

    @pl.when(z0 < depth - 1)
    def _():
        greet(along(1, 0), seg)

    @pl.when(helps)
    def _():
        greet(clients[0], seg)

    @pl.when(helps_two)
    def _():
        greet(clients[1], seg)

    keep = pltpu.make_async_copy(prop.at[0, seg], mats.at[seg], precv.at[seg])
    keep.start()
    begin = pltpu.make_async_copy(src.at[seg], first, fsem)
    begin.start()

    below = jnp.where(z0 > 0, 1, 0)
    is_late = jnp.where(late, 1, 0)
    pl.semaphore_wait(barrier, len(near) + 1 + below + is_late)

    def send(to, start, length):
        cut = pl.ds(start, length)
        pltpu.make_async_remote_copy(
            prop.at[0, to, :, cut], mats.at[seg, :, cut], psend, precv.at[seg],
            device_id=(freq, to), device_id_type=MESH).start()

    def tell(devices, sem):
        for to in devices:
            pl.semaphore_signal(sem, 1, device_id=(freq, to), device_id_type=MESH)

    def send_farthest(p, length):
        @pl.when(jnp.logical_not(late))
        def _():
            send(plane[0], p * length, length)

        if DIRECT > p * length:
            @pl.when(late)
            def _():
                send(plane[0], p * length, min(length, DIRECT - p * length))

    def send_relayed():
        @pl.when(late)
        def _():
            pl.semaphore_wait(go, 1)
            cut = pl.ds(DIRECT, modes - DIRECT)
            pltpu.make_async_remote_copy(
                prop.at[0, plane[0], :, cut], relay.at[slot], psend, relay_recv.at[slot],
                device_id=(helper, plane[0]), device_id_type=MESH).start()

    tell(near, plane_sem.at[0])
    for to in near:
        send(to, 0, HEAD_NEAR)
    @pl.when(z0 > 0)
    def _():
        pl.semaphore_signal(hello, 1, device_id=(along(-1, 0), seg), device_id_type=MESH)

    @pl.when(late)
    def _():
        pl.semaphore_signal(ask, 1, device_id=(helper, seg), device_id_type=MESH)

    @pl.when(z0 == depth - 1)
    def _():
        pl.semaphore_signal(hello, 1, device_id=(along(1, 0), seg), device_id_type=MESH)


    pl.semaphore_wait(plane_sem.at[0], len(near))
    tell(second, plane_sem.at[1])
    for to in second:
        send(to, 0, HEAD_SECOND)
    pl.semaphore_wait(plane_sem.at[1], len(second))
    half = modes // 2
    for p in range(2):
        send_farthest(p, half)
        for to in plane[1:n_far]:
            send(to, p * half, half)
        if p == 0:
            send_relayed()
    if HEAD_SECOND < modes:
        for to in second:
            send(to, HEAD_SECOND, modes - HEAD_SECOND)
    if HEAD_NEAR < modes:
        for to in near:
            send(to, HEAD_NEAR, modes - HEAD_NEAR)

    forward = [
        pltpu.make_async_remote_copy(
            relay.at[i], mats.at[plane[0], :, pl.ds(DIRECT, modes - DIRECT)], relay_send.at[i],
            precv.at[plane[0]], device_id=(client, seg), device_id_type=MESH)
        for i, client in enumerate(clients)
    ]

    @pl.when(helps_two)
    def _():
        pl.semaphore_wait(ask, 2)
        for client in clients:
            pl.semaphore_signal(go, 1, device_id=(client, seg), device_id_type=MESH)

    @pl.when(jnp.logical_and(helps, jnp.logical_not(helps_two)))
    def _():
        pl.semaphore_wait(ask, 1)
        pl.semaphore_signal(go, 1, device_id=(clients[0], seg), device_id_type=MESH)

    width = CORES * n_seg
    t = lax.broadcasted_iota(jnp.int32, (n_time, modes), 0)
    lane = lax.broadcasted_iota(jnp.int32, (n_time, modes), 1)
    column, block = lax.rem(lane, width), lane // width
    f = column // 2 + freq * n_seg
    phase = lax.rem(t * f, n_time).astype(F32) * (2.0 * np.pi / n_time)
    scale = 1.0 / np.sqrt(np.float32(n_time))
    twiddle = jnp.where(lax.rem(column, 2) == 0, jnp.cos(phase), -jnp.sin(phase)) * scale
    t_hi, t_mid, t_lo = (v.astype(F32) for v in split3(twiddle))
    zero = jnp.zeros_like(twiddle)
    table[:, :modes] = jnp.where(block < 2, t_hi, t_mid).astype(BF16)
    table[:, modes:] = jnp.where(
        block == 0, t_hi, jnp.where(block == 1, t_lo, zero)).astype(BF16)

    for i, here in enumerate((helps, helps_two)):
        @pl.when(here)
        def _(i=i):
            pltpu.make_async_copy(relay.at[i], relay.at[i], relay_recv.at[i]).wait()
            forward[i].start()

    @pl.when(z0 == 0)
    def _():
        pl.semaphore_wait(hello, 2)

    @pl.when(jnp.logical_and(z0 > 0, z0 < depth - 1))
    def _():
        pl.semaphore_wait(hello, 1)

    rounds = depth // 2
    for r in range(rounds):
        for to in near_line:
            pl.semaphore_signal(line_sem.at[r], 1, device_id=(to, seg), device_id_type=MESH)
        pl.semaphore_wait(line_sem.at[r], len(near_line))

    eye = lax.broadcasted_iota(jnp.int32, (modes, modes), 0) == lax.broadcasted_iota(
        jnp.int32, (modes, modes), 1)

    def to_row(value):
        return jnp.sum(jnp.where(eye, value, 0.0), axis=0, keepdims=True)

    def amp_copy(s):
        return pltpu.make_async_remote_copy(
            own.at[s], amp.at[seg], asend.at[s], arecv,
            device_id=(freq, s), device_id_type=MESH)

    def fetch(s):
        pltpu.make_async_copy(mats.at[s], mats.at[s], precv.at[s]).wait()
        return mats[s, 0], mats[s, 1]

    def give(s, re, im):
        own[s, 0:1, :] = re
        own[s, 1:2, :] = im

        @pl.when(s != seg)
        def _():
            amp_copy(s).start()

    def step(s, vec):
        re, im = vec
        p_re, p_im = fetch(s)
        n_re = to_row(jnp.sum(p_re * re - p_im * im, axis=1, keepdims=True))
        n_im = to_row(jnp.sum(p_re * im + p_im * re, axis=1, keepdims=True))
        give(s, n_re, n_im)
        return n_re, n_im

    begin.wait()
    lax.fori_loop(0, n_seg, step, (first[0:1, :], first[1:2, :]))
    amp[seg] = own[seg]

    pltpu.make_async_copy(amp.at[pl.ds(0, n_seg - 1)], amp.at[pl.ds(0, n_seg - 1)], arecv).wait()
    a_hi, a_mid, a_lo = split3(amp[...].reshape(2 * n_seg, modes))
    none = jnp.zeros_like(a_hi)
    stacked = jnp.concatenate([a_hi, a_mid, a_hi, a_mid, a_lo, a_hi, none, none], axis=0)
    part[...] = jnp.dot(table[...], stacked, preferred_element_type=F32).reshape(
        n_freq, rows, modes)

    outs = []
    half = depth // 2
    for dz in sorted(range(1 - half, half + 1), key=lambda d: -abs(d)):
        for dc in range(CORES):
            if (dz, dc) == (0, 0):
                continue
            to = along(dz, dc)
            i = len(outs)
            copy = pltpu.make_async_remote_copy(
                part.at[to], got.at[i], wsend.at[i], wrecv,
                device_id=(to, seg), device_id_type=MESH)
            copy.start()
            outs.append(copy)

    amp_out[0] = amp[...]
    sent = mats.at[pl.ds(0, n_seg - 1)]
    pltpu.make_async_copy(sent, sent, psend).wait()

    def drain(s, carry):
        @pl.when(s != seg)
        def _():
            amp_copy(s).wait_send()

        return carry

    lax.fori_loop(0, n_seg, drain, 0)
    pltpu.make_async_copy(got, got, wrecv).wait()
    wave_out[:, 0, :] = part[freq] + jnp.sum(got[...], axis=0)
    for copy in outs:
        copy.wait_send()

    for i, here in enumerate((helps, helps_two)):
        @pl.when(here)
        def _(i=i):
            forward[i].wait_send()


def local(propagators, source_modes):
    n_seg, n_freq = lax.axis_size("seg"), lax.axis_size("freq")
    _, group, _, modes, _ = propagators.shape
    dma, plain = pltpu.SemaphoreType.DMA, pltpu.SemaphoreType.REGULAR
    amps, waves = pl.pallas_call(
        functools.partial(kernel, n_seg, n_freq),
        out_shape=(
            jax.ShapeDtypeStruct((1, group, 2, modes), F32),
            jax.ShapeDtypeStruct((group, 1, modes), F32),
        ),
        in_specs=[pl.BlockSpec(memory_space=pltpu.HBM)] * 2,
        out_specs=(pl.BlockSpec(memory_space=pltpu.VMEM),) * 2,
        scratch_shapes=[
            pltpu.VMEM((n_seg, 2, modes, modes), F32),
            pltpu.VMEM((n_seg, 2, modes), F32),
            pltpu.VMEM((n_seg, 2, modes), F32),
            pltpu.VMEM((n_freq, group, modes), F32),
            pltpu.VMEM((n_freq - 1, group, modes), F32),
            pltpu.VMEM((n_freq * group, 2 * modes), BF16),
            pltpu.VMEM((2, modes), F32),
            dma,
            dma((n_seg,)),
            dma((n_seg,)),
            dma,
            dma((n_freq - 1,)),
            dma,
            dma,
            plain((n_freq // CORES // 2,)),
            plain((2,)),
            pltpu.VMEM((2, 2, modes - DIRECT, modes), F32),
            dma((2,)),
            dma((2,)),
            plain,
            plain,
            plain,
        ],
        compiler_params=pltpu.CompilerParams(
            collective_id=0, has_side_effects=True, vmem_limit_bytes=54500 << 10
        ),
    )(*(pltpu.with_memory_space_constraint(v, pltpu.HBM) for v in (propagators, source_modes)))

    def hand_on(a, w, a_out, w_out):
        a_out[...] = a[...]
        w_out[...] = w[...]

    return pl.pallas_call(
        hand_on,
        out_shape=(
            jax.ShapeDtypeStruct(amps.shape, F32),
            jax.ShapeDtypeStruct(waves.shape, F32),
        ),
        compiler_params=pltpu.CompilerParams(vmem_limit_bytes=4 << 20),
    )(amps, waves)


def solution(mesh):
    placed = (P("seg", "freq", None, None, None), P("freq", None, None))
    return jax.shard_map(
        local,
        mesh=mesh,
        in_specs=placed,
        out_specs=(P("seg", "freq", None, None), P("freq", "seg", None)),
        check_vma=False,
    )
```

```python
import functools

import jax
import jax.numpy as jnp
import numpy as np
from jax import lax
from jax.experimental import pallas as pl
from jax.experimental.pallas import tpu as pltpu
from jax.sharding import PartitionSpec as P

MESH = pl.DeviceIdType.MESH
F32 = jnp.float32
BF16 = jnp.bfloat16
SIDE = 4
CORES = 2
PLANE = (
    (2, 2), (1, 2), (2, 1), (-1, 2), (2, -1), (1, 1), (-1, -1), (1, -1), (-1, 1),
    (2, 0), (0, 2), (1, 0), (0, 1), (-1, 0), (0, -1),
)
DIRECT = 48
HEAD_NEAR = 96
HEAD_SECOND = 64


def split3(value):
    hi = value.astype(BF16)
    rest = value - hi.astype(F32)
    mid = rest.astype(BF16)
    return hi, mid, (rest - mid.astype(F32)).astype(BF16)


def kernel(n_seg, n_freq, prop, src, amp_out, wave_out, mats, own, amp, part, got, table, first,
           psend, precv, asend, arecv, wsend, wrecv, fsem, line_sem, plane_sem, relay,
           relay_send, relay_recv, hello, ask, go):
    seg = lax.axis_index("seg")
    freq = lax.axis_index("freq")
    modes = mats.shape[-1]
    rows = wave_out.shape[0]
    n_time = rows * n_freq
    x0, y0 = lax.div(seg, SIDE), lax.rem(seg, SIDE)
    depth = n_freq // CORES
    z0, core = lax.div(freq, CORES), lax.rem(freq, CORES)
    across = {d: lax.rem(x0 + d + SIDE, SIDE) * SIDE for d in (1, -1, 2)} | {0: x0 * SIDE}
    down = {d: lax.rem(y0 + d + SIDE, SIDE) for d in (1, -1, 2)} | {0: y0}

    def at(offset):
        dx, dy = offset
        return across[dx] + down[dy]

    def along(dz, dc):
        return lax.rem(z0 + dz + depth, depth) * CORES + lax.rem(core + dc, CORES)

    plane = [at(offset) for offset in PLANE]
    n_far, n_near = 5, 4
    near, second = plane[-n_near:], plane[n_far:-n_near]
    near_line = [along(0, 1), along(1, 0), along(-1, 0)]
    middle = depth // 2
    late = z0 >= middle
    helps = z0 < middle - 1
    helps_two = z0 == 0
    slot = jnp.where(z0 == middle, 1, 0)
    helper = jnp.where(z0 == middle, 0, depth - 1 - z0) * CORES + core
    clients = ((depth - 1 - z0) * CORES + core, middle * CORES + core)

    barrier = pltpu.get_barrier_semaphore()

    def greet(line, plane_to):
        pl.semaphore_signal(barrier, 1, device_id=(line, plane_to), device_id_type=MESH)

    for to in near:
        greet(freq, to)
    greet(along(0, 1), seg)

    @pl.when(z0 < depth - 1)
    def _():
        greet(along(1, 0), seg)

    @pl.when(helps)
    def _():
        greet(clients[0], seg)

    @pl.when(helps_two)
    def _():
        greet(clients[1], seg)

    keep = pltpu.make_async_copy(prop.at[0, seg], mats.at[seg], precv.at[seg])
    keep.start()
    begin = pltpu.make_async_copy(src.at[seg], first, fsem)
    begin.start()

    below = jnp.where(z0 > 0, 1, 0)
    is_late = jnp.where(late, 1, 0)
    pl.semaphore_wait(barrier, len(near) + 1 + below + is_late)

    def send(to, start, length):
        cut = pl.ds(start, length)
        pltpu.make_async_remote_copy(
            prop.at[0, to, :, cut], mats.at[seg, :, cut], psend, precv.at[seg],
            device_id=(freq, to), device_id_type=MESH).start()

    def tell(devices, sem):
        for to in devices:
            pl.semaphore_signal(sem, 1, device_id=(freq, to), device_id_type=MESH)

    def send_farthest(p, length):
        @pl.when(jnp.logical_not(late))
        def _():
            send(plane[0], p * length, length)

        if DIRECT > p * length:
            @pl.when(late)
            def _():
                send(plane[0], p * length, min(length, DIRECT - p * length))

    def send_relayed():
        @pl.when(late)
        def _():
            pl.semaphore_wait(go, 1)
            cut = pl.ds(DIRECT, modes - DIRECT)
            pltpu.make_async_remote_copy(
                prop.at[0, plane[0], :, cut], relay.at[slot], psend, relay_recv.at[slot],
                device_id=(helper, plane[0]), device_id_type=MESH).start()

    tell(near, plane_sem.at[0])
    for to in near:
        send(to, 0, HEAD_NEAR)
    @pl.when(z0 > 0)
    def _():
        pl.semaphore_signal(hello, 1, device_id=(along(-1, 0), seg), device_id_type=MESH)

    @pl.when(late)
    def _():
        pl.semaphore_signal(ask, 1, device_id=(helper, seg), device_id_type=MESH)

    @pl.when(z0 == depth - 1)
    def _():
        pl.semaphore_signal(hello, 1, device_id=(along(1, 0), seg), device_id_type=MESH)


    pl.semaphore_wait(plane_sem.at[0], len(near))
    tell(second, plane_sem.at[1])
    for to in second:
        send(to, 0, HEAD_SECOND)
    pl.semaphore_wait(plane_sem.at[1], len(second))
    half = modes // 2
    for p in range(2):
        send_farthest(p, half)
        for to in plane[1:n_far]:
            send(to, p * half, half)
        if p == 0:
            send_relayed()
    if HEAD_SECOND < modes:
        for to in second:
            send(to, HEAD_SECOND, modes - HEAD_SECOND)
    if HEAD_NEAR < modes:
        for to in near:
            send(to, HEAD_NEAR, modes - HEAD_NEAR)

    forward = [
        pltpu.make_async_remote_copy(
            relay.at[i], mats.at[plane[0], :, pl.ds(DIRECT, modes - DIRECT)], relay_send.at[i],
            precv.at[plane[0]], device_id=(client, seg), device_id_type=MESH)
        for i, client in enumerate(clients)
    ]

    @pl.when(helps_two)
    def _():
        pl.semaphore_wait(ask, 2)
        for client in clients:
            pl.semaphore_signal(go, 1, device_id=(client, seg), device_id_type=MESH)

    @pl.when(jnp.logical_and(helps, jnp.logical_not(helps_two)))
    def _():
        pl.semaphore_wait(ask, 1)
        pl.semaphore_signal(go, 1, device_id=(clients[0], seg), device_id_type=MESH)

    width = CORES * n_seg
    t = lax.broadcasted_iota(jnp.int32, (n_time, modes), 0)
    lane = lax.broadcasted_iota(jnp.int32, (n_time, modes), 1)
    column, block = lax.rem(lane, width), lane // width
    f = column // 2 + freq * n_seg
    phase = lax.rem(t * f, n_time).astype(F32) * (2.0 * np.pi / n_time)
    scale = 1.0 / np.sqrt(np.float32(n_time))
    twiddle = jnp.where(lax.rem(column, 2) == 0, jnp.cos(phase), -jnp.sin(phase)) * scale
    t_hi, t_mid, t_lo = (v.astype(F32) for v in split3(twiddle))
    zero = jnp.zeros_like(twiddle)
    table[:, :modes] = jnp.where(block < 2, t_hi, t_mid).astype(BF16)
    table[:, modes:] = jnp.where(
        block == 0, t_hi, jnp.where(block == 1, t_lo, zero)).astype(BF16)

    for i, here in enumerate((helps, helps_two)):
        @pl.when(here)
        def _(i=i):
            pltpu.make_async_copy(relay.at[i], relay.at[i], relay_recv.at[i]).wait()
            forward[i].start()

    @pl.when(z0 == 0)
    def _():
        pl.semaphore_wait(hello, 2)

    @pl.when(jnp.logical_and(z0 > 0, z0 < depth - 1))
    def _():
        pl.semaphore_wait(hello, 1)

    rounds = depth // 2
    for r in range(rounds):
        for to in near_line:
            pl.semaphore_signal(line_sem.at[r], 1, device_id=(to, seg), device_id_type=MESH)
        pl.semaphore_wait(line_sem.at[r], len(near_line))

    eye = lax.broadcasted_iota(jnp.int32, (modes, modes), 0) == lax.broadcasted_iota(
        jnp.int32, (modes, modes), 1)

    def to_row(value):
        return jnp.sum(jnp.where(eye, value, 0.0), axis=0, keepdims=True)

    def amp_copy(s):
        return pltpu.make_async_remote_copy(
            own.at[s], amp.at[seg], asend.at[s], arecv,
            device_id=(freq, s), device_id_type=MESH)

    def fetch(s):
        pltpu.make_async_copy(mats.at[s], mats.at[s], precv.at[s]).wait()
        return mats[s, 0], mats[s, 1]

    def give(s, re, im):
        own[s, 0:1, :] = re
        own[s, 1:2, :] = im

        @pl.when(s != seg)
        def _():
            amp_copy(s).start()

    def step(s, vec):
        re, im = vec
        p_re, p_im = fetch(s)
        n_re = to_row(jnp.sum(p_re * re - p_im * im, axis=1, keepdims=True))
        n_im = to_row(jnp.sum(p_re * im + p_im * re, axis=1, keepdims=True))
        give(s, n_re, n_im)
        return n_re, n_im

    begin.wait()
    lax.fori_loop(0, n_seg, step, (first[0:1, :], first[1:2, :]), unroll=2)
    amp[seg] = own[seg]

    pltpu.make_async_copy(amp.at[pl.ds(0, n_seg - 1)], amp.at[pl.ds(0, n_seg - 1)], arecv).wait()
    a_hi, a_mid, a_lo = split3(amp[...].reshape(2 * n_seg, modes))
    none = jnp.zeros_like(a_hi)
    stacked = jnp.concatenate([a_hi, a_mid, a_hi, a_mid, a_lo, a_hi, none, none], axis=0)
    part[...] = jnp.dot(table[...], stacked, preferred_element_type=F32).reshape(
        n_freq, rows, modes)

    outs = []
    half = depth // 2
    for dz in sorted(range(1 - half, half + 1), key=lambda d: -abs(d)):
        for dc in range(CORES):
            if (dz, dc) == (0, 0):
                continue
            to = along(dz, dc)
            i = len(outs)
            copy = pltpu.make_async_remote_copy(
                part.at[to], got.at[i], wsend.at[i], wrecv,
                device_id=(to, seg), device_id_type=MESH)
            copy.start()
            outs.append(copy)

    amp_out[0] = amp[...]
    sent = mats.at[pl.ds(0, n_seg - 1)]
    pltpu.make_async_copy(sent, sent, psend).wait()

    def drain(s, carry):
        @pl.when(s != seg)
        def _():
            amp_copy(s).wait_send()

        return carry

    lax.fori_loop(0, n_seg, drain, 0)
    pltpu.make_async_copy(got, got, wrecv).wait()
    wave_out[:, 0, :] = part[freq] + jnp.sum(got[...], axis=0)
    for copy in outs:
        copy.wait_send()

    for i, here in enumerate((helps, helps_two)):
        @pl.when(here)
        def _(i=i):
            forward[i].wait_send()


def local(propagators, source_modes):
    n_seg, n_freq = lax.axis_size("seg"), lax.axis_size("freq")
    _, group, _, modes, _ = propagators.shape
    dma, plain = pltpu.SemaphoreType.DMA, pltpu.SemaphoreType.REGULAR
    amps, waves = pl.pallas_call(
        functools.partial(kernel, n_seg, n_freq),
        out_shape=(
            jax.ShapeDtypeStruct((1, group, 2, modes), F32),
            jax.ShapeDtypeStruct((group, 1, modes), F32),
        ),
        in_specs=[pl.BlockSpec(memory_space=pltpu.HBM)] * 2,
        out_specs=(pl.BlockSpec(memory_space=pltpu.VMEM),) * 2,
        scratch_shapes=[
            pltpu.VMEM((n_seg, 2, modes, modes), F32),
            pltpu.VMEM((n_seg, 2, modes), F32),
            pltpu.VMEM((n_seg, 2, modes), F32),
            pltpu.VMEM((n_freq, group, modes), F32),
            pltpu.VMEM((n_freq - 1, group, modes), F32),
            pltpu.VMEM((n_freq * group, 2 * modes), BF16),
            pltpu.VMEM((2, modes), F32),
            dma,
            dma((n_seg,)),
            dma((n_seg,)),
            dma,
            dma((n_freq - 1,)),
            dma,
            dma,
            plain((n_freq // CORES // 2,)),
            plain((2,)),
            pltpu.VMEM((2, 2, modes - DIRECT, modes), F32),
            dma((2,)),
            dma((2,)),
            plain,
            plain,
            plain,
        ],
        compiler_params=pltpu.CompilerParams(
            collective_id=0, has_side_effects=True, vmem_limit_bytes=54500 << 10
        ),
    )(*(pltpu.with_memory_space_constraint(v, pltpu.HBM) for v in (propagators, source_modes)))

    def hand_on(a, w, a_out, w_out):
        a_out[...] = a[...]
        w_out[...] = w[...]

    return pl.pallas_call(
        hand_on,
        out_shape=(
            jax.ShapeDtypeStruct(amps.shape, F32),
            jax.ShapeDtypeStruct(waves.shape, F32),
        ),
        compiler_params=pltpu.CompilerParams(vmem_limit_bytes=4 << 20),
    )(amps, waves)


def solution(mesh):
    placed = (P("seg", "freq", None, None, None), P("freq", None, None))
    return jax.shard_map(
        local,
        mesh=mesh,
        in_specs=placed,
        out_specs=(P("seg", "freq", None, None), P("freq", "seg", None)),
        check_vma=False,
    )
```

```python
import functools

import jax
import jax.numpy as jnp
import numpy as np
from jax import lax
from jax.experimental import pallas as pl
from jax.experimental.pallas import tpu as pltpu
from jax.sharding import PartitionSpec as P

MESH = pl.DeviceIdType.MESH
F32 = jnp.float32
BF16 = jnp.bfloat16
SIDE = 4
CORES = 2
PLANE = (
    (2, 2), (1, 2), (2, 1), (-1, 2), (2, -1), (1, 1), (-1, -1), (1, -1), (-1, 1),
    (2, 0), (0, 2), (1, 0), (0, 1), (-1, 0), (0, -1),
)
DIRECT = 48
HEAD_NEAR = 96
HEAD_SECOND = 64


def split3(value):
    hi = value.astype(BF16)
    rest = value - hi.astype(F32)
    mid = rest.astype(BF16)
    return hi, mid, (rest - mid.astype(F32)).astype(BF16)


def kernel(n_seg, n_freq, prop, src, amp_out, wave_out, mats, own, amp, part, got, table, first,
           psend, precv, asend, arecv, wsend, wrecv, fsem, line_sem, plane_sem, relay,
           relay_send, relay_recv, hello, ask, go):
    seg = lax.axis_index("seg")
    freq = lax.axis_index("freq")
    modes = mats.shape[-1]
    rows = wave_out.shape[0]
    n_time = rows * n_freq
    x0, y0 = lax.div(seg, SIDE), lax.rem(seg, SIDE)
    depth = n_freq // CORES
    z0, core = lax.div(freq, CORES), lax.rem(freq, CORES)
    across = {d: lax.rem(x0 + d + SIDE, SIDE) * SIDE for d in (1, -1, 2)} | {0: x0 * SIDE}
    down = {d: lax.rem(y0 + d + SIDE, SIDE) for d in (1, -1, 2)} | {0: y0}

    def at(offset):
        dx, dy = offset
        return across[dx] + down[dy]

    def along(dz, dc):
        return lax.rem(z0 + dz + depth, depth) * CORES + lax.rem(core + dc, CORES)

    plane = [at(offset) for offset in PLANE]
    n_far, n_near = 5, 4
    near, second = plane[-n_near:], plane[n_far:-n_near]
    near_line = [along(0, 1), along(1, 0), along(-1, 0)]
    middle = depth // 2
    late = z0 >= middle
    helps = z0 < middle - 1
    helps_two = z0 == 0
    slot = jnp.where(z0 == middle, 1, 0)
    helper = jnp.where(z0 == middle, 0, depth - 1 - z0) * CORES + core
    clients = ((depth - 1 - z0) * CORES + core, middle * CORES + core)

    barrier = pltpu.get_barrier_semaphore()

    def greet(line, plane_to):
        pl.semaphore_signal(barrier, 1, device_id=(line, plane_to), device_id_type=MESH)

    for to in near:
        greet(freq, to)
    greet(along(0, 1), seg)

    @pl.when(z0 < depth - 1)
    def _():
        greet(along(1, 0), seg)

    @pl.when(helps)
    def _():
        greet(clients[0], seg)

    @pl.when(helps_two)
    def _():
        greet(clients[1], seg)

    keep = pltpu.make_async_copy(prop.at[0, seg], mats.at[seg], precv.at[seg])
    keep.start()
    begin = pltpu.make_async_copy(src.at[seg], first, fsem)
    begin.start()

    below = jnp.where(z0 > 0, 1, 0)
    is_late = jnp.where(late, 1, 0)
    pl.semaphore_wait(barrier, len(near) + 1 + below + is_late)

    def send(to, start, length):
        cut = pl.ds(start, length)
        pltpu.make_async_remote_copy(
            prop.at[0, to, :, cut], mats.at[seg, :, cut], psend, precv.at[seg],
            device_id=(freq, to), device_id_type=MESH).start()

    def tell(devices, sem):
        for to in devices:
            pl.semaphore_signal(sem, 1, device_id=(freq, to), device_id_type=MESH)

    def send_farthest(p, length):
        @pl.when(jnp.logical_not(late))
        def _():
            send(plane[0], p * length, length)

        if DIRECT > p * length:
            @pl.when(late)
            def _():
                send(plane[0], p * length, min(length, DIRECT - p * length))

    def send_relayed():
        @pl.when(late)
        def _():
            pl.semaphore_wait(go, 1)
            cut = pl.ds(DIRECT, modes - DIRECT)
            pltpu.make_async_remote_copy(
                prop.at[0, plane[0], :, cut], relay.at[slot], psend, relay_recv.at[slot],
                device_id=(helper, plane[0]), device_id_type=MESH).start()

    tell(near, plane_sem.at[0])
    for to in near:
        send(to, 0, HEAD_NEAR)
    @pl.when(z0 > 0)
    def _():
        pl.semaphore_signal(hello, 1, device_id=(along(-1, 0), seg), device_id_type=MESH)

    @pl.when(late)
    def _():
        pl.semaphore_signal(ask, 1, device_id=(helper, seg), device_id_type=MESH)

    @pl.when(z0 == depth - 1)
    def _():
        pl.semaphore_signal(hello, 1, device_id=(along(1, 0), seg), device_id_type=MESH)


    pl.semaphore_wait(plane_sem.at[0], len(near))
    tell(second, plane_sem.at[1])
    for to in second:
        send(to, 0, HEAD_SECOND)
    pl.semaphore_wait(plane_sem.at[1], len(second))
    half = modes // 2
    rest = (modes - HEAD_SECOND) // 2
    for p in range(2):
        send_farthest(p, half)
        for to in plane[1:n_far]:
            send(to, p * half, half)
        if p == 0:
            send_relayed()
        for to in second:
            send(to, HEAD_SECOND + p * rest, rest)
    for to in near:
        send(to, HEAD_NEAR, modes - HEAD_NEAR)

    forward = [
        pltpu.make_async_remote_copy(
            relay.at[i], mats.at[plane[0], :, pl.ds(DIRECT, modes - DIRECT)], relay_send.at[i],
            precv.at[plane[0]], device_id=(client, seg), device_id_type=MESH)
        for i, client in enumerate(clients)
    ]

    @pl.when(helps_two)
    def _():
        pl.semaphore_wait(ask, 2)
        for client in clients:
            pl.semaphore_signal(go, 1, device_id=(client, seg), device_id_type=MESH)

    @pl.when(jnp.logical_and(helps, jnp.logical_not(helps_two)))
    def _():
        pl.semaphore_wait(ask, 1)
        pl.semaphore_signal(go, 1, device_id=(clients[0], seg), device_id_type=MESH)

    width = CORES * n_seg
    t = lax.broadcasted_iota(jnp.int32, (n_time, modes), 0)
    lane = lax.broadcasted_iota(jnp.int32, (n_time, modes), 1)
    column, block = lax.rem(lane, width), lane // width
    f = column // 2 + freq * n_seg
    phase = lax.rem(t * f, n_time).astype(F32) * (2.0 * np.pi / n_time)
    scale = 1.0 / np.sqrt(np.float32(n_time))
    twiddle = jnp.where(lax.rem(column, 2) == 0, jnp.cos(phase), -jnp.sin(phase)) * scale
    t_hi, t_mid, t_lo = (v.astype(F32) for v in split3(twiddle))
    zero = jnp.zeros_like(twiddle)
    table[:, :modes] = jnp.where(block < 2, t_hi, t_mid).astype(BF16)
    table[:, modes:] = jnp.where(
        block == 0, t_hi, jnp.where(block == 1, t_lo, zero)).astype(BF16)

    for i, here in enumerate((helps, helps_two)):
        @pl.when(here)
        def _(i=i):
            pltpu.make_async_copy(relay.at[i], relay.at[i], relay_recv.at[i]).wait()
            forward[i].start()

    @pl.when(z0 == 0)
    def _():
        pl.semaphore_wait(hello, 2)

    @pl.when(jnp.logical_and(z0 > 0, z0 < depth - 1))
    def _():
        pl.semaphore_wait(hello, 1)

    rounds = depth // 2
    for r in range(rounds):
        for to in near_line:
            pl.semaphore_signal(line_sem.at[r], 1, device_id=(to, seg), device_id_type=MESH)
        pl.semaphore_wait(line_sem.at[r], len(near_line))

    eye = lax.broadcasted_iota(jnp.int32, (modes, modes), 0) == lax.broadcasted_iota(
        jnp.int32, (modes, modes), 1)

    def to_row(value):
        return jnp.sum(jnp.where(eye, value, 0.0), axis=0, keepdims=True)

    def amp_copy(s):
        return pltpu.make_async_remote_copy(
            own.at[s], amp.at[seg], asend.at[s], arecv,
            device_id=(freq, s), device_id_type=MESH)

    def fetch(s):
        pltpu.make_async_copy(mats.at[s], mats.at[s], precv.at[s]).wait()
        return mats[s, 0], mats[s, 1]

    def give(s, re, im):
        own[s, 0:1, :] = re
        own[s, 1:2, :] = im

        @pl.when(s != seg)
        def _():
            amp_copy(s).start()

    def step(s, vec):
        re, im = vec
        p_re, p_im = fetch(s)
        n_re = to_row(jnp.sum(p_re * re - p_im * im, axis=1, keepdims=True))
        n_im = to_row(jnp.sum(p_re * im + p_im * re, axis=1, keepdims=True))
        give(s, n_re, n_im)
        return n_re, n_im

    begin.wait()
    lax.fori_loop(0, n_seg, step, (first[0:1, :], first[1:2, :]))
    amp[seg] = own[seg]

    pltpu.make_async_copy(amp.at[pl.ds(0, n_seg - 1)], amp.at[pl.ds(0, n_seg - 1)], arecv).wait()
    a_hi, a_mid, a_lo = split3(amp[...].reshape(2 * n_seg, modes))
    none = jnp.zeros_like(a_hi)
    stacked = jnp.concatenate([a_hi, a_mid, a_hi, a_mid, a_lo, a_hi, none, none], axis=0)
    part[...] = jnp.dot(table[...], stacked, preferred_element_type=F32).reshape(
        n_freq, rows, modes)

    outs = []
    half = depth // 2
    for dz in sorted(range(1 - half, half + 1), key=lambda d: -abs(d)):
        for dc in range(CORES):
            if (dz, dc) == (0, 0):
                continue
            to = along(dz, dc)
            i = len(outs)
            copy = pltpu.make_async_remote_copy(
                part.at[to], got.at[i], wsend.at[i], wrecv,
                device_id=(to, seg), device_id_type=MESH)
            copy.start()
            outs.append(copy)

    amp_out[0] = amp[...]
    sent = mats.at[pl.ds(0, n_seg - 1)]
    pltpu.make_async_copy(sent, sent, psend).wait()

    def drain(s, carry):
        @pl.when(s != seg)
        def _():
            amp_copy(s).wait_send()

        return carry

    lax.fori_loop(0, n_seg, drain, 0)
    pltpu.make_async_copy(got, got, wrecv).wait()
    wave_out[:, 0, :] = part[freq] + jnp.sum(got[...], axis=0)
    for copy in outs:
        copy.wait_send()

    for i, here in enumerate((helps, helps_two)):
        @pl.when(here)
        def _(i=i):
            forward[i].wait_send()


def local(propagators, source_modes):
    n_seg, n_freq = lax.axis_size("seg"), lax.axis_size("freq")
    _, group, _, modes, _ = propagators.shape
    dma, plain = pltpu.SemaphoreType.DMA, pltpu.SemaphoreType.REGULAR
    amps, waves = pl.pallas_call(
        functools.partial(kernel, n_seg, n_freq),
        out_shape=(
            jax.ShapeDtypeStruct((1, group, 2, modes), F32),
            jax.ShapeDtypeStruct((group, 1, modes), F32),
        ),
        in_specs=[pl.BlockSpec(memory_space=pltpu.HBM)] * 2,
        out_specs=(pl.BlockSpec(memory_space=pltpu.VMEM),) * 2,
        scratch_shapes=[
            pltpu.VMEM((n_seg, 2, modes, modes), F32),
            pltpu.VMEM((n_seg, 2, modes), F32),
            pltpu.VMEM((n_seg, 2, modes), F32),
            pltpu.VMEM((n_freq, group, modes), F32),
            pltpu.VMEM((n_freq - 1, group, modes), F32),
            pltpu.VMEM((n_freq * group, 2 * modes), BF16),
            pltpu.VMEM((2, modes), F32),
            dma,
            dma((n_seg,)),
            dma((n_seg,)),
            dma,
            dma((n_freq - 1,)),
            dma,
            dma,
            plain((n_freq // CORES // 2,)),
            plain((2,)),
            pltpu.VMEM((2, 2, modes - DIRECT, modes), F32),
            dma((2,)),
            dma((2,)),
            plain,
            plain,
            plain,
        ],
        compiler_params=pltpu.CompilerParams(
            collective_id=0, has_side_effects=True, vmem_limit_bytes=54500 << 10
        ),
    )(*(pltpu.with_memory_space_constraint(v, pltpu.HBM) for v in (propagators, source_modes)))

    def hand_on(a, w, a_out, w_out):
        a_out[...] = a[...]
        w_out[...] = w[...]

    return pl.pallas_call(
        hand_on,
        out_shape=(
            jax.ShapeDtypeStruct(amps.shape, F32),
            jax.ShapeDtypeStruct(waves.shape, F32),
        ),
        compiler_params=pltpu.CompilerParams(vmem_limit_bytes=4 << 20),
    )(amps, waves)


def solution(mesh):
    placed = (P("seg", "freq", None, None, None), P("freq", None, None))
    return jax.shard_map(
        local,
        mesh=mesh,
        in_specs=placed,
        out_specs=(P("seg", "freq", None, None), P("freq", "seg", None)),
        check_vma=False,
    )
```
